256 devices in a mesh: dom: 128 (over z, x, y), feat: 2 (over core).
Axes of the slice: x: 4, y: 4, z: 8, core: 2. Of those that a mesh axis runs over, the one named last changes fastest.
Arguments:
- features: bfloat16 [524288, 256], P('dom', 'feat'), may hold values from -6 to 6
- self_weight: bfloat16 [256, 256], P('feat'), may hold values from -0.375 to 0.375
- neighbor_weight: bfloat16 [256, 256], P('feat'), may hold values from -0.375 to 0.375
- tile_values: bfloat16 [20480, 128, 128], P('dom'), may hold values from 0 to 1
- tile_row: int32 [20480], P('dom'), may hold values from 0 to 31
- tile_owner: int32 [20480], P('dom'), may hold values from 0 to 127
- send_tile: int32 [16384], P('dom'), may hold values from 0 to 31
- tile_count: int32 [128], P('dom'), may hold values from 26 to 160, as said below
- hub_panel: bfloat16 [524288, 256], P('dom'), may hold values from 0 to 1
- hub_rows: int32 [256], P('dom'), may hold values from 0 to 4095
- cotangent: bfloat16 [524288, 256], P('dom', 'feat'), may hold values from -6 to 6
Outputs:
- layer_out: bfloat16 [524288, 256], P('dom', 'feat')
- self_grad: float32 [256, 256], P('feat')
- neighbor_grad: float32 [256, 256], P('feat')
- input_grad: float32 [524288, 256], P('dom', 'feat')
The draws below stay inside these ranges and needn't reach their ends.
Inputs may be any that keep to these rules, and one draw needn't show every extreme that they name: `tile_count`: one partition has exactly 160 live slots in every draw.
All inputs are finite; a program needn't handle non-finite values.
Results may differ from the reference program's by a relative error of at most 0.011.
The reference program's roundings to bfloat16 on the way count: a program that leaves them out, or rounds other values in their place, can miss the bound.
Values may be sent and summed in bfloat16 or wider, within the bound.
No kernel may reach another device: no remote copies, remote signals or barrier semaphores. Data moves between devices by JAX's collectives and lax.ppermute only.
A program may use at most 128 MiB of HBM per device.

```python
import math
import jax
import jax.numpy as jnp
from jax import lax

D = 256
TILE = 128
HUB_DEV = 2
V_DEV = 4096
TILES_DEV = 32
TILE_CAP = 160
HUBS = 256
V = 524288
N_DOM = 128


def draw_tile_owner(key, part):
    keys = jax.random.split(key, N_DOM)
    orders = jax.vmap(lambda single: jax.random.permutation(single, N_DOM))(keys)
    picks = jnp.arange(TILE_CAP) % N_DOM
    return orders[:, picks].reshape(N_DOM * TILE_CAP).astype(jnp.int32)


def draw_tile_count(key, part):
    counts = jax.random.randint(key, (N_DOM,), TILE_CAP // 6, TILE_CAP // 2 + 1)
    chosen = jax.random.randint(jax.random.fold_in(key, 7), (), 0, N_DOM)
    return jnp.where(jnp.arange(N_DOM) == chosen, TILE_CAP, counts).astype(jnp.int32)


def set_ends(result, stream_key, smallest, top_value):
    spot = [jax.random.randint(jax.random.fold_in(stream_key, axis), (), 0, length) for axis, length in enumerate(result.shape)]
    widest = result.shape.index(max(result.shape))
    next_to = spot[:widest] + [(spot[widest] + 1) % result.shape[widest]] + spot[widest + 1:]
    return result.at[tuple(spot)].set(smallest).at[tuple(next_to)].set(top_value)


def block_scale(rng, shape, shards, smallest, largest):
    loudness, own = 1.0, jax.random.fold_in(rng, 6)
    for dim, parts in shards:
        draws = jnp.exp(jax.random.uniform(jax.random.fold_in(own, dim), (parts,), jnp.float32, smallest / len(shards), largest / len(shards)))
        loudness = loudness * jnp.repeat(draws, shape[dim] // parts).reshape([-1 if axis == dim else 1 for axis in range(len(shape))])
    return loudness


def normal_values(key, dims, spread, reach, shards=(), kind=jnp.bfloat16):
    array = spread * jax.random.normal(key, dims, jnp.float32)
    if shards:
        array = array * block_scale(key, dims, shards, -0.22, 0.18)
    return jnp.clip(array, -reach, reach).astype(kind)


def setup_inputs(seed: int = 0) -> dict:
    seeds = jax.random.split(jax.random.key(seed), 12)
    features = normal_values(seeds[0], (V, D), 1.0, 6.0, ((0, 128), (1, 2)))
    self_weight = normal_values(seeds[1], (D, D), D ** -0.5, 0.375, ((0, 2),))
    neighbor_weight = normal_values(seeds[2], (D, D), D ** -0.5, 0.375, ((0, 2),))
    tile_values = jnp.clip(1.0 * jax.random.uniform(seeds[3], (N_DOM * TILE_CAP, TILE, TILE), jnp.float32) ** block_scale(seeds[3], (N_DOM * TILE_CAP, TILE, TILE), ((0, 128),), -0.2, 0.2), 0.0, 1.0).astype(jnp.bfloat16)
    tile_row = set_ends(jax.random.randint(seeds[4], (N_DOM * TILE_CAP,), 0, TILES_DEV), jax.random.fold_in(seeds[4], 1), 0, TILES_DEV - 1).astype(jnp.int32)
    tile_owner = draw_tile_owner(jax.random.fold_in(seeds[11], 71), 0)
    send_tile = set_ends(jax.random.randint(seeds[6], (N_DOM * N_DOM,), 0, TILES_DEV), jax.random.fold_in(seeds[6], 1), 0, TILES_DEV - 1).astype(jnp.int32)
    tile_count = draw_tile_count(jax.random.fold_in(seeds[11], 71), 0)
    hub_panel = jnp.clip(1.0 * jax.random.uniform(seeds[8], (V, HUBS), jnp.float32) ** block_scale(seeds[8], (V, HUBS), ((0, 128),), -0.2, 0.2), 0.0, 1.0).astype(jnp.bfloat16)
    hub_rows = set_ends(jax.random.randint(seeds[9], (HUBS,), 0, V_DEV), jax.random.fold_in(seeds[9], 1), 0, V_DEV - 1).astype(jnp.int32)
    cotangent = normal_values(seeds[10], (V, D), 1.0, 6.0, ((0, 128), (1, 2)))
    return {"features": features, "self_weight": self_weight, "neighbor_weight": neighbor_weight, "tile_values": tile_values, "tile_row": tile_row, "tile_owner": tile_owner, "send_tile": send_tile, "tile_count": tile_count, "hub_panel": hub_panel, "hub_rows": hub_rows, "cotangent": cotangent}


def reference(features, self_weight, neighbor_weight, tile_values, tile_row, tile_owner, send_tile, tile_count, hub_panel, hub_rows, cotangent):
    tiles_dev = V_DEV // TILE
    highest = lax.Precision.HIGHEST
    feature_tiles = features.reshape(N_DOM, tiles_dev, TILE, D)
    values_all = tile_values.reshape(N_DOM, TILE_CAP, TILE, TILE)
    rows_all = tile_row.reshape(N_DOM, TILE_CAP)
    owners_all = tile_owner.reshape(N_DOM, TILE_CAP)
    sends = send_tile.reshape(N_DOM, N_DOM)
    panels = hub_panel.reshape(N_DOM, V_DEV, HUBS)
    local_feats = features.reshape(N_DOM, V_DEV, D)
    local_cot = cotangent.reshape(N_DOM, V_DEV, D)
    hub_owner = (jnp.arange(HUBS) // HUB_DEV).astype(jnp.int32)
    hub_global = (hub_owner * V_DEV + hub_rows).astype(jnp.int32)
    hub_feats = features[hub_global].astype(jnp.float32)
    every_owner = jnp.arange(N_DOM).astype(jnp.int32)

    def step(carry, index):
        remote, hub_acc, self_acc, neigh_acc = carry
        values = values_all[index].astype(jnp.float32)
        rows = rows_all[index]
        owners = owners_all[index]
        live = (jnp.arange(TILE_CAP) < tile_count[index]).astype(jnp.float32)
        col_tiles = sends[owners, index]
        columns = feature_tiles[owners, col_tiles].astype(jnp.float32)
        products = jnp.einsum('kij,kjf->kif', values, columns, precision=highest) * live[:, None, None]
        panel = panels[index].astype(jnp.float32)
        sums = jax.ops.segment_sum(products, rows, num_segments=tiles_dev).reshape(V_DEV, D)
        sums = sums + jnp.dot(panel, hub_feats, precision=highest)
        tile_squares = lax.optimization_barrier(jnp.sum(values * values, axis=2)) * live[:, None]
        squares = jax.ops.segment_sum(tile_squares, rows, num_segments=tiles_dev).reshape(V_DEV)
        squares = squares + lax.optimization_barrier(jnp.sum(panel * panel, axis=1))
        inverse_norm = lax.rsqrt(1.0 + squares)
        aggregate = (sums * inverse_norm[:, None]).astype(jnp.bfloat16)
        x_here = local_feats[index]
        preact = jnp.dot(x_here, self_weight, preferred_element_type=jnp.float32) + jnp.dot(aggregate, neighbor_weight, preferred_element_type=jnp.float32)
        layer_part = jnp.maximum(preact, 0.0).astype(jnp.bfloat16)
        slopes = jnp.where(preact > 0, local_cot[index].astype(jnp.float32), 0.0).astype(jnp.bfloat16)
        self_acc = self_acc + jnp.dot(x_here.T, slopes, preferred_element_type=jnp.float32)
        neigh_acc = neigh_acc + jnp.dot(aggregate.T, slopes, preferred_element_type=jnp.float32)
        direct = jnp.dot(slopes, self_weight.T, preferred_element_type=jnp.float32)
        agg_slopes = (jnp.dot(slopes, neighbor_weight.T, preferred_element_type=jnp.float32) * inverse_norm[:, None]).astype(jnp.bfloat16)
        slope_tiles = agg_slopes.reshape(tiles_dev, TILE, D)[rows].astype(jnp.float32)
        tile_back = jnp.einsum('kji,kjf->kif', values, slope_tiles, precision=highest) * live[:, None, None]
        owner_terms = jax.ops.segment_sum(tile_back, owners, num_segments=N_DOM).astype(jnp.bfloat16).astype(jnp.float32)
        remote = remote.at[every_owner, sends[:, index]].add(owner_terms)
        hub_acc = hub_acc + jnp.dot(panel.T, agg_slopes.astype(jnp.float32), precision=highest)
        return ((remote, hub_acc, self_acc, neigh_acc), (layer_part, direct))
    start = (jnp.zeros((N_DOM, tiles_dev, TILE, D), jnp.float32), jnp.zeros((HUBS, D), jnp.float32), jnp.zeros((D, D), jnp.float32), jnp.zeros((D, D), jnp.float32))
    final, stacked = lax.scan(step, start, jnp.arange(N_DOM, dtype=jnp.int32))
    remote, hub_acc, self_acc, neigh_acc = final
    layer_parts, directs = stacked
    factor = 1.0 / math.sqrt(N_DOM * V_DEV)
    input_grad = directs.reshape(N_DOM * V_DEV, D) + remote.reshape(N_DOM * V_DEV, D)
    input_grad = input_grad.at[hub_global].add(hub_acc)
    return (layer_parts.reshape(N_DOM * V_DEV, D), self_acc * factor, neigh_acc * factor, input_grad)
```

```python
import math

import jax
import jax.numpy as jnp
from jax import lax
from jax.experimental import pallas as pl
from jax.experimental.pallas import tpu as pltpu
from jax.sharding import PartitionSpec as P

F32 = jnp.float32
BF16 = jnp.bfloat16
MIB = 1 << 20


def dot(a, b, dims):
    return lax.dot_general(a, b, (dims, ((), ())), preferred_element_type=F32)


NN = ((1,), (0,))
NT = ((1,), (1,))
TN = ((0,), (0,))


def params(mib, steps):
    return pltpu.CompilerParams(
        dimension_semantics=("arbitrary",) * steps, vmem_limit_bytes=mib * MIB
    )


def pack_kernel(send, hubs, feat, out, hub_rows):
    step = pl.program_id(0)
    per_step, edge = out.shape[0], out.shape[1] - 8

    @pl.when(step == 0)
    def _():
        hub_rows[...] = jnp.zeros_like(hub_rows)
        for j in range(2):
            row = hubs[j]
            base = pl.multiple_of((row // 16) * 16, 16)
            block = feat[pl.ds(base, 16), :].astype(F32)
            here = lax.broadcasted_iota(jnp.int32, block.shape, 0) == row - base
            hub_rows[j : j + 1, :] = jnp.sum(
                jnp.where(here, block, 0.0), axis=0, keepdims=True
            )

    extra = hub_rows[...].astype(BF16)
    for i in range(per_step):
        start = pl.multiple_of(send[step * per_step + i] * edge, edge)
        out[i, :edge, :] = feat[pl.ds(start, edge), :]
        out[i, edge:, :] = extra


def pack(features, send_tile, hub_rows, edge):
    rows, width = features.shape
    parts = send_tile.shape[0]
    per_step = 16
    return pl.pallas_call(
        pack_kernel,
        name="pack",
        out_shape=jax.ShapeDtypeStruct((parts, edge + 8, width), BF16),
        grid_spec=pltpu.PrefetchScalarGridSpec(
            num_scalar_prefetch=2,
            grid=(parts // per_step,),
            in_specs=[pl.BlockSpec((rows, width), lambda g, *_: (0, 0))],
            out_specs=pl.BlockSpec((per_step, edge + 8, width), lambda g, *_: (g, 0, 0)),
            scratch_shapes=[pltpu.VMEM((8, width), F32)],
        ),
        compiler_params=params(16, 1),
    )(send_tile, hub_rows, features)


def prepare_kernel(
    row, count, order, first, second, kinds, values, panel, inv, flipped, pairs, squares
):
    step, steps = pl.program_id(0), pl.num_programs(0)
    edge = values.shape[1]
    slots, duos = flipped.shape[0], pairs.shape[0]

    @pl.when(step == 0)
    def _():
        squares[...] = jnp.zeros_like(squares)

    @pl.loop(0, slots)
    def _(i):
        k = step * slots + i
        flipped[i] = values[order[k]].T
        tile = values[k].astype(F32)
        live = (k < count[0]).astype(F32)
        start = pl.multiple_of(row[k] * edge, edge)
        squares[pl.ds(start, edge), :] += tile * tile * live

    @pl.loop(0, duos)
    def _(i):
        p = step * duos + i
        has_first = (kinds[p] > 0).astype(BF16)
        has_second = (kinds[p] > 1).astype(BF16)
        pairs[i, :, :edge] = values[first[p]] * has_first
        pairs[i, :, edge:] = values[second[p]] * has_second

    @pl.when(step == steps - 1)
    def _():
        @pl.loop(0, squares.shape[0] // edge)
        def _(t):
            at = pl.ds(pl.multiple_of(t * edge, edge), edge)
            wide = panel[at, :].astype(F32)
            wide = wide * wide
            half = wide.shape[1] // 2
            total = jnp.sum(
                squares[at, :] + wide[:, :half] + wide[:, half:], axis=1, keepdims=True
            )
            inv[at, :] = jnp.broadcast_to(lax.rsqrt(1.0 + total), (edge, inv.shape[1]))


def prepare(row, count, order, first, second, kinds, values, panel, duos):
    slots, edge, _ = values.shape
    rows, hubs = panel.shape
    steps = 4
    whole = lambda g, *_: (0, 0)
    return pl.pallas_call(
        prepare_kernel,
        name="prepare",
        out_shape=(
            jax.ShapeDtypeStruct((rows, edge), F32),
            jax.ShapeDtypeStruct((slots, edge, edge), BF16),
            jax.ShapeDtypeStruct((duos, edge, 2 * edge), BF16),
        ),
        grid_spec=pltpu.PrefetchScalarGridSpec(
            num_scalar_prefetch=6,
            grid=(steps,),
            in_specs=[
                pl.BlockSpec((slots, edge, edge), lambda g, *_: (0, 0, 0)),
                pl.BlockSpec((rows, hubs), whole),
            ],
            out_specs=(
                pl.BlockSpec((rows, edge), whole),
                pl.BlockSpec((slots // steps, edge, edge), lambda g, *_: (g, 0, 0)),
                pl.BlockSpec((duos // steps, edge, 2 * edge), lambda g, *_: (g, 0, 0)),
            ),
            scratch_shapes=[pltpu.VMEM((rows, edge), F32)],
        ),
        compiler_params=params(40, 1),
        cost_estimate=pl.CostEstimate(
            flops=60_000_000_000, bytes_accessed=40_000_000, transcendentals=0
        ),
    )(row, count, order, first, second, kinds, values, panel)


def gather_kernel(row, owner_a, owner_b, n_duos, pairs, incoming, panel, inv, out, sums):
    step, steps = pl.program_id(0), pl.num_programs(0)
    duos, edge, _ = pairs.shape
    parts = incoming.shape[0]

    @pl.when(step == 0)
    def _():
        tail = incoming[:, edge:, :].reshape(parts * 8, incoming.shape[2])
        h = lax.broadcasted_iota(jnp.int32, (2 * parts, parts * 8), 0)
        r = lax.broadcasted_iota(jnp.int32, (2 * parts, parts * 8), 1)
        pick = (r == (h // 2) * 8 + h % 2).astype(F32).astype(BF16)
        hub_feats = dot(pick, tail, NN).astype(BF16)

        @pl.loop(0, sums.shape[0] // 512)
        def _(t):
            at = pl.ds(pl.multiple_of(t * 512, 512), 512)
            sums[at, :] = dot(panel[at, :], hub_feats, NN)

    @pl.when(step * duos < n_duos[0])
    def _():
        products = []
        for i in range(duos):
            p = step * duos + i
            columns = jnp.concatenate(
                [incoming[owner_a[p], :edge, :], incoming[owner_b[p], :edge, :]], axis=0
            )
            products.append(dot(pairs[i], columns, NN))
        for i in range(duos):
            start = pl.multiple_of(row[step * duos + i] * edge, edge)
            sums[pl.ds(start, edge), :] += products[i]

    @pl.when(step == steps - 1)
    def _():
        @pl.loop(0, sums.shape[0] // 512)
        def _(t):
            at = pl.ds(pl.multiple_of(t * 512, 512), 512)
            out[at, :] = (sums[at, :] * inv[at, :]).astype(BF16)


def gather(row, owner_a, owner_b, n_duos, pairs, incoming, panel, inv):
    duos, edge, _ = pairs.shape
    rows, hubs = panel.shape
    per_step = 8
    whole = lambda g, *_: (0, 0)

    def block(g, row, owner_a, owner_b, n_duos):
        return (jnp.minimum(g, (n_duos[0] - 1) // per_step), 0, 0)

    return pl.pallas_call(
        gather_kernel,
        name="gather",
        out_shape=jax.ShapeDtypeStruct((rows, edge), BF16),
        grid_spec=pltpu.PrefetchScalarGridSpec(
            num_scalar_prefetch=4,
            grid=(duos // per_step,),
            in_specs=[
                pl.BlockSpec((per_step, edge, 2 * edge), block),
                pl.BlockSpec(incoming.shape, lambda g, *_: (0, 0, 0)),
                pl.BlockSpec((rows, hubs), whole),
                pl.BlockSpec((rows, edge), whole),
            ],
            out_specs=pl.BlockSpec((rows, edge), whole),
            scratch_shapes=[pltpu.VMEM((rows, edge), F32)],
        ),
        compiler_params=params(40, 1),
    )(row, owner_a, owner_b, n_duos, pairs, incoming, panel, inv)


def middle_kernel(
    feat, feat_peer, agg, agg_peer, cot, cot_peer, inv, panel, own_w, nbr_w,
    layer, slopes_out, agg_slopes_out, extra, hub_acc, grad_acc,
):
    step, steps = pl.program_id(0), pl.num_programs(0)
    half = feat.shape[1]
    x = feat[...]
    a = agg[...]
    preact = dot(jnp.concatenate([x, feat_peer[...]], axis=1), own_w[...], NN) + dot(
        jnp.concatenate([a, agg_peer[...]], axis=1), nbr_w[...], NN
    )
    layer[...] = jnp.maximum(preact[:, :half], 0.0).astype(BF16)
    cotangent = jnp.concatenate([cot[...], cot_peer[...]], axis=1).astype(F32)
    slopes = jnp.where(preact > 0, cotangent, 0.0).astype(BF16)
    slopes_out[...] = slopes
    agg_slopes = (dot(slopes, nbr_w[:half, :], NT) * inv[...]).astype(BF16)
    agg_slopes_out[...] = agg_slopes
    hub = dot(panel[...], agg_slopes, TN)
    grads = dot(jnp.concatenate([x, a], axis=1), slopes, TN)

    @pl.when(step == 0)
    def _():
        hub_acc[...] = hub
        grad_acc[...] = grads

    @pl.when(step > 0)
    def _():
        hub_acc[...] += hub
        grad_acc[...] += grads

    @pl.when(step == steps - 1)
    def _():
        n = half
        extra[...] = jnp.zeros_like(extra)
        for j in range(2):
            extra[pl.ds(j, n, stride=8), :] = hub_acc[pl.ds(j, n, stride=2), :]
            for c in range(2):
                extra[pl.ds(2 + 2 * j + c, n, stride=8), :] = grad_acc[
                    j * n : (j + 1) * n, c * n : (c + 1) * n
                ]


def middle(feat, feat_peer, agg, agg_peer, cot, cot_peer, inv, panel, own_w, nbr_w):
    rows, half = feat.shape
    hubs = panel.shape[1]
    block = 512
    by_row = lambda width: pl.BlockSpec((block, width), lambda g: (g, 0))
    whole = lambda shape: pl.BlockSpec(shape, lambda g: (0, 0))
    return pl.pallas_call(
        middle_kernel,
        name="middle",
        out_shape=(
            jax.ShapeDtypeStruct((rows, half), BF16),
            jax.ShapeDtypeStruct((rows, 2 * half), BF16),
            jax.ShapeDtypeStruct((rows, half), BF16),
            jax.ShapeDtypeStruct((8 * half, half), F32),
        ),
        grid=(rows // block,),
        in_specs=[by_row(half)] * 7
        + [by_row(hubs), whole(own_w.shape), whole(nbr_w.shape)],
        out_specs=(by_row(half), by_row(2 * half), by_row(half), whole((8 * half, half))),
        scratch_shapes=[
            pltpu.VMEM((hubs, half), F32),
            pltpu.VMEM((2 * half, 2 * half), F32),
        ],
        compiler_params=params(32, 1),
    )(feat, feat_peer, agg, agg_peer, cot, cot_peer, inv, panel, own_w, nbr_w)


def back_kernel(order_row, order_owner, same, live, count, flipped, slopes, *rest):
    extra = rest[0] if len(rest) == 3 else None
    out, carry = rest[-2:]
    step = pl.program_id(0)
    slots, part, edge = flipped.shape

    @pl.when(step == 0)
    def _():
        out[:, :part, :] = jnp.zeros((out.shape[0], part, out.shape[2]), out.dtype)
        carry[...] = jnp.zeros_like(carry)
        if extra is not None:
            out[:, part:, :] = extra[...].astype(BF16)

    @pl.when(step * slots < count[0])
    def _():
        products = []
        for i in range(slots):
            start = pl.multiple_of(order_row[step * slots + i] * edge, edge)
            products.append(dot(flipped[i], slopes[pl.ds(start, edge), :], NN))
        total = carry[...]
        for i in range(slots):
            k = step * slots + i
            total = products[i] * live[k].astype(F32) + total * same[k].astype(F32)
            out[order_owner[k], :part, :] = total.astype(BF16)
        carry[...] = total


def back(order_row, order_owner, same, live, count, flipped, slopes, extra, side):
    slots, edge, _ = flipped.shape
    rows, half = slopes.shape
    part = edge // 2
    parts = 128 if extra is None else extra.shape[0]
    per_step = 16

    def block(g, order_row, order_owner, same, live, count):
        return (jnp.minimum(g, (count[0] - 1) // per_step), side, 0)

    height = part + (8 if extra is not None else 0)
    in_specs = [
        pl.BlockSpec((per_step, part, edge), block),
        pl.BlockSpec((rows, half), lambda g, *_: (0, 0)),
    ]
    args = [flipped, slopes]
    if extra is not None:
        in_specs.append(pl.BlockSpec(extra.shape, lambda g, *_: (0, 0, 0)))
        args.append(extra)
    return pl.pallas_call(
        back_kernel,
        name=f"back_{side}",
        out_shape=jax.ShapeDtypeStruct((parts, height, half), BF16),
        grid_spec=pltpu.PrefetchScalarGridSpec(
            num_scalar_prefetch=5,
            grid=(slots // per_step,),
            in_specs=in_specs,
            out_specs=pl.BlockSpec((parts, height, half), lambda g, *_: (0, 0, 0)),
            scratch_shapes=[pltpu.VMEM((part, half), F32)],
        ),
        compiler_params=params(32, 1),
    )(order_row, order_owner, same, live, count, *args)


def finish_first_kernel(send, hubs, slopes, own_w, returned, out, share):
    parts, height, half = returned.shape
    tiles, edge = out.shape[0], out.shape[1]
    part = height - 8

    @pl.loop(0, tiles)
    def _(t):
        at = pl.ds(pl.multiple_of(t * edge, edge), edge)
        out[t] = dot(slopes[at, :], own_w[...], NT)

    total = jnp.zeros((8, half), F32)
    for p in range(parts):
        out[send[p], :part, :] += returned[p, :part, :].astype(F32)
        total = total + returned[p, part:, :].astype(F32)
    share[...] = total
    for j in range(2):
        row = hubs[j]
        tile, inside = row // edge, row % edge
        base = pl.multiple_of((inside // 8) * 8, 8)
        here = lax.broadcasted_iota(jnp.int32, (8, half), 0) == inside - base
        out[tile, pl.ds(base, 8), :] += jnp.where(here, total[j : j + 1, :], 0.0)


def finish_first(send_tile, hub_rows, slopes, own_w, returned, edge):
    rows = slopes.shape[0]
    half = returned.shape[2]
    smem = pl.BlockSpec(memory_space=pltpu.SMEM)
    vmem = pl.BlockSpec(memory_space=pltpu.VMEM)
    return pl.pallas_call(
        finish_first_kernel,
        name="finish_first",
        out_shape=(
            jax.ShapeDtypeStruct((rows // edge, edge, half), F32),
            jax.ShapeDtypeStruct((8, half), F32),
        ),
        in_specs=[smem, smem, vmem, vmem, vmem],
        out_specs=(vmem, vmem),
        compiler_params=pltpu.CompilerParams(vmem_limit_bytes=24 * MIB),
    )(send_tile, hub_rows, slopes, own_w, returned)


def finish_second_kernel(send, returned, before, out):
    out[...] = before[...]
    for p in range(returned.shape[0]):
        out[send[p]] += returned[p].astype(F32)


def finish_second(send_tile, returned, before):
    tiles, edge, half = before.shape
    spec = pl.BlockSpec((tiles, edge // 2, half), lambda g, *_: (0, 1, 0))
    return pl.pallas_call(
        finish_second_kernel,
        name="finish_second",
        out_shape=jax.ShapeDtypeStruct(before.shape, F32),
        grid_spec=pltpu.PrefetchScalarGridSpec(
            num_scalar_prefetch=1,
            grid=(1,),
            in_specs=[pl.BlockSpec(returned.shape, lambda g, *_: (0, 0, 0)), spec],
            out_specs=spec,
        ),
        input_output_aliases={2: 0},
        compiler_params=params(24, 1),
    )(send_tile, returned, before)


def plan(tile_row, tile_owner, tile_count, tiles, parts):
    slots = tile_row.shape[0]
    index = jnp.arange(slots, dtype=jnp.int32)
    live = index < tile_count[0]
    earlier = index[None, :] < index[:, None]
    pick = lambda where, what: jnp.sum(jnp.where(where, what, 0), axis=1, dtype=jnp.int32)

    key = jnp.where(live, tile_owner, parts)
    before = (key[None, :] < key[:, None]) | ((key[None, :] == key[:, None]) & earlier)
    rank = jnp.sum(before, axis=1, dtype=jnp.int32)
    last = jnp.minimum(index, tile_count[0] - 1)
    at = rank[None, :] == last[:, None]
    order = pick(at, index[None, :])
    order_row = pick(at, tile_row[None, :])
    order_owner = pick(at, tile_owner[None, :])
    same = jnp.concatenate([jnp.zeros((1,), jnp.int32), (order_owner[1:] == order_owner[:-1]).astype(jnp.int32)])
    live_int = live.astype(jnp.int32)

    mates = live[None, :] & (tile_row[None, :] == tile_row[:, None])
    inside = jnp.sum(mates & earlier, axis=1, dtype=jnp.int32)
    rows = jnp.arange(tiles, dtype=jnp.int32)
    per_row = jnp.sum(live[None, :] & (tile_row[None, :] == rows[:, None]), axis=1, dtype=jnp.int32)
    row_pairs = (per_row + 1) // 2
    lower = jnp.sum(
        jnp.where(rows[None, :] < tile_row[:, None], row_pairs[None, :], 0), axis=1, dtype=jnp.int32
    )
    pair = jnp.where(live, lower + inside // 2, -1)
    duos = (slots + tiles) // 2
    p = jnp.arange(duos, dtype=jnp.int32)
    is_first = (pair[None, :] == p[:, None]) & (inside[None, :] % 2 == 0)
    is_second = (pair[None, :] == p[:, None]) & (inside[None, :] % 2 == 1)
    first = pick(is_first, index[None, :])
    second = pick(is_second, index[None, :])
    owner_a = pick(is_first, tile_owner[None, :])
    owner_b = pick(is_second, tile_owner[None, :])
    pair_row = pick(is_first, tile_row[None, :])
    kinds = pick(is_first, 1) + pick(is_second, 1)
    n_duos = jnp.sum(row_pairs, dtype=jnp.int32).reshape(1)
    return (
        (order, order_row, order_owner, same, live_int),
        (first, second, kinds, pair_row, owner_a, owner_b, n_duos),
        duos,
    )


def exchange(block):
    return lax.all_to_all(block, "dom", split_axis=0, concat_axis=0, tiled=True)


def swap(block):
    return lax.ppermute(block, "feat", [(0, 1), (1, 0)])


def shards(
    features,
    self_weight,
    neighbor_weight,
    tile_values,
    tile_row,
    tile_owner,
    send_tile,
    tile_count,
    hub_panel,
    hub_rows,
    cotangent,
):
    rows_dev, half = features.shape
    tile_edge = tile_values.shape[1]
    tiles_dev = rows_dev // tile_edge
    dom_size = lax.axis_size("dom")
    core = lax.axis_index("feat")

    outgoing = pack(features, send_tile, hub_rows, tile_edge)
    incoming = exchange(outgoing)

    def own_first(w):
        return jnp.where(core == 0, w, jnp.concatenate([w[:, half:], w[:, :half]], axis=1))

    weights = own_first(jnp.concatenate([self_weight, neighbor_weight], axis=0))
    peer_weights = swap(weights)
    peer_weights = jnp.concatenate([peer_weights[:, half:], peer_weights[:, :half]], axis=1)
    own_w = jnp.concatenate([weights[:half], peer_weights[:half]], axis=0)
    nbr_w = jnp.concatenate([weights[half:], peer_weights[half:]], axis=0)
    feat_peer = swap(features)
    cot_peer = swap(cotangent)

    by_owner, by_row, duos = plan(tile_row, tile_owner, tile_count, tiles_dev, dom_size)
    order, order_row, order_owner, same, live = by_owner
    first, second, kinds, pair_row, owner_a, owner_b, n_duos = by_row
    inv, flipped, pairs = prepare(
        tile_row, tile_count, order, first, second, kinds, tile_values, hub_panel, duos
    )

    aggregate = gather(pair_row, owner_a, owner_b, n_duos, pairs, incoming, hub_panel, inv)
    agg_peer = swap(aggregate)
    layer_out, slopes, agg_slopes, extra = middle(
        features, feat_peer, aggregate, agg_peer, cotangent, cot_peer, inv, hub_panel, own_w, nbr_w
    )
    extra = extra.reshape(dom_size, 8, half)
    back_args = (order_row, order_owner, same, live, tile_count, flipped, agg_slopes)
    returned_a = exchange(back(*back_args, extra, 0))
    returned_b = exchange(back(*back_args, None, 1))

    partial_grad, share = finish_first(
        send_tile, hub_rows, slopes, own_w[:half], returned_a, tile_edge
    )
    grads = exchange(jnp.broadcast_to(share[None, 2:6], (dom_size, 4, half)))
    input_grad = finish_second(send_tile, returned_b, partial_grad).reshape(rows_dev, half)

    grads = grads * (1.0 / math.sqrt(rows_dev * dom_size))
    sides = [jnp.concatenate([grads[:, 2 * j], grads[:, 2 * j + 1]], axis=1) for j in range(2)]
    self_grad, neighbor_grad = (own_first(side) for side in sides)
    return (layer_out, self_grad, neighbor_grad, input_grad)


def solution(mesh):
    placed = (
        P("dom", "feat"),
        P("feat", None),
        P("feat", None),
        P("dom", None, None),
        P("dom"),
        P("dom"),
        P("dom"),
        P("dom"),
        P("dom", None),
        P("dom"),
        P("dom", "feat"),
    )
    return jax.shard_map(
        shards,
        mesh=mesh,
        in_specs=placed,
        out_specs=(P("dom", "feat"), P("feat", None), P("feat", None), P("dom", "feat")),
        check_vma=False,
    )
```

```python
import math

import jax
import jax.numpy as jnp
from jax import lax
from jax.experimental import pallas as pl
from jax.experimental.pallas import tpu as pltpu
from jax.sharding import PartitionSpec as P

F32 = jnp.float32
BF16 = jnp.bfloat16
MIB = 1 << 20


def dot(a, b, dims):
    return lax.dot_general(a, b, (dims, ((), ())), preferred_element_type=F32)


NN = ((1,), (0,))
NT = ((1,), (1,))
TN = ((0,), (0,))


def params(mib, steps):
    return pltpu.CompilerParams(
        dimension_semantics=("arbitrary",) * steps, vmem_limit_bytes=mib * MIB
    )


def pack_kernel(send, hubs, feat, out, hub_rows):
    step = pl.program_id(0)
    per_step, edge = out.shape[0], out.shape[1] - 8

    @pl.when(step == 0)
    def _():
        hub_rows[...] = jnp.zeros_like(hub_rows)
        for j in range(2):
            row = hubs[j]
            base = pl.multiple_of((row // 16) * 16, 16)
            block = feat[pl.ds(base, 16), :].astype(F32)
            here = lax.broadcasted_iota(jnp.int32, block.shape, 0) == row - base
            hub_rows[j : j + 1, :] = jnp.sum(
                jnp.where(here, block, 0.0), axis=0, keepdims=True
            )

    extra = hub_rows[...].astype(BF16)
    for i in range(per_step):
        start = pl.multiple_of(send[step * per_step + i] * edge, edge)
        out[i, :edge, :] = feat[pl.ds(start, edge), :]
        out[i, edge:, :] = extra


def pack(features, send_tile, hub_rows, edge):
    rows, width = features.shape
    parts = send_tile.shape[0]
    per_step = 16
    return pl.pallas_call(
        pack_kernel,
        name="pack",
        out_shape=jax.ShapeDtypeStruct((parts, edge + 8, width), BF16),
        grid_spec=pltpu.PrefetchScalarGridSpec(
            num_scalar_prefetch=2,
            grid=(parts // per_step,),
            in_specs=[pl.BlockSpec((rows, width), lambda g, *_: (0, 0))],
            out_specs=pl.BlockSpec((per_step, edge + 8, width), lambda g, *_: (g, 0, 0)),
            scratch_shapes=[pltpu.VMEM((8, width), F32)],
        ),
        compiler_params=params(58, 1),
    )(send_tile, hub_rows, features)


def prepare_kernel(
    row, count, order, first, second, kinds, values, panel, inv, flipped, pairs, squares
):
    step, steps = pl.program_id(0), pl.num_programs(0)
    edge = values.shape[1]
    slots, duos = flipped.shape[0], pairs.shape[0]

    @pl.when(step == 0)
    def _():
        squares[...] = jnp.zeros_like(squares)

    @pl.loop(0, slots)
    def _(i):
        k = step * slots + i
        flipped[i] = values[order[k]].T
        tile = values[k].astype(F32)
        live = (k < count[0]).astype(F32)
        start = pl.multiple_of(row[k] * edge, edge)
        squares[pl.ds(start, edge), :] += tile * tile * live

    @pl.loop(0, duos)
    def _(i):
        p = step * duos + i
        has_first = (kinds[p] > 0).astype(BF16)
        has_second = (kinds[p] > 1).astype(BF16)
        pairs[i, :, :edge] = values[first[p]] * has_first
        pairs[i, :, edge:] = values[second[p]] * has_second

    @pl.when(step == steps - 1)
    def _():
        @pl.loop(0, squares.shape[0] // edge)
        def _(t):
            at = pl.ds(pl.multiple_of(t * edge, edge), edge)
            wide = panel[at, :].astype(F32)
            wide = wide * wide
            half = wide.shape[1] // 2
            total = jnp.sum(
                squares[at, :] + wide[:, :half] + wide[:, half:], axis=1, keepdims=True
            )
            inv[at, :] = jnp.broadcast_to(lax.rsqrt(1.0 + total), (edge, inv.shape[1]))


def prepare(row, count, order, first, second, kinds, values, panel, duos):
    slots, edge, _ = values.shape
    rows, hubs = panel.shape
    steps = 4
    whole = lambda g, *_: (0, 0)
    return pl.pallas_call(
        prepare_kernel,
        name="prepare",
        out_shape=(
            jax.ShapeDtypeStruct((rows, edge), F32),
            jax.ShapeDtypeStruct((slots, edge, edge), BF16),
            jax.ShapeDtypeStruct((duos, edge, 2 * edge), BF16),
        ),
        grid_spec=pltpu.PrefetchScalarGridSpec(
            num_scalar_prefetch=6,
            grid=(steps,),
            in_specs=[
                pl.BlockSpec((slots, edge, edge), lambda g, *_: (0, 0, 0)),
                pl.BlockSpec((rows, hubs), whole),
            ],
            out_specs=(
                pl.BlockSpec((rows, edge), whole),
                pl.BlockSpec((slots // steps, edge, edge), lambda g, *_: (g, 0, 0)),
                pl.BlockSpec((duos // steps, edge, 2 * edge), lambda g, *_: (g, 0, 0)),
            ),
            scratch_shapes=[pltpu.VMEM((rows, edge), F32)],
        ),
        compiler_params=params(40, 1),
        cost_estimate=pl.CostEstimate(
            flops=60_000_000_000, bytes_accessed=40_000_000, transcendentals=0
        ),
    )(row, count, order, first, second, kinds, values, panel)


def gather_kernel(row, owner_a, owner_b, n_duos, pairs, incoming, panel, inv, out, sums):
    step, steps = pl.program_id(0), pl.num_programs(0)
    duos, edge, _ = pairs.shape
    parts = incoming.shape[0]

    @pl.when(step == 0)
    def _():
        tail = incoming[:, edge:, :].reshape(parts * 8, incoming.shape[2])
        h = lax.broadcasted_iota(jnp.int32, (2 * parts, parts * 8), 0)
        r = lax.broadcasted_iota(jnp.int32, (2 * parts, parts * 8), 1)
        pick = (r == (h // 2) * 8 + h % 2).astype(F32).astype(BF16)
        hub_feats = dot(pick, tail, NN).astype(BF16)

        @pl.loop(0, sums.shape[0] // 512)
        def _(t):
            at = pl.ds(pl.multiple_of(t * 512, 512), 512)
            sums[at, :] = dot(panel[at, :], hub_feats, NN)

    @pl.when(step * duos < n_duos[0])
    def _():
        products = []
        for i in range(duos):
            p = step * duos + i
            columns = jnp.concatenate(
                [incoming[owner_a[p], :edge, :], incoming[owner_b[p], :edge, :]], axis=0
            )
            products.append(dot(pairs[i], columns, NN))
        for i in range(duos):
            start = pl.multiple_of(row[step * duos + i] * edge, edge)
            sums[pl.ds(start, edge), :] += products[i]

    @pl.when(step == steps - 1)
    def _():
        @pl.loop(0, sums.shape[0] // 512)
        def _(t):
            at = pl.ds(pl.multiple_of(t * 512, 512), 512)
            out[at, :] = (sums[at, :] * inv[at, :]).astype(BF16)


def gather(row, owner_a, owner_b, n_duos, pairs, incoming, panel, inv):
    duos, edge, _ = pairs.shape
    rows, hubs = panel.shape
    per_step = 16
    whole = lambda g, *_: (0, 0)

    def block(g, row, owner_a, owner_b, n_duos):
        return (jnp.minimum(g, (n_duos[0] - 1) // per_step), 0, 0)

    return pl.pallas_call(
        gather_kernel,
        name="gather",
        out_shape=jax.ShapeDtypeStruct((rows, edge), BF16),
        grid_spec=pltpu.PrefetchScalarGridSpec(
            num_scalar_prefetch=4,
            grid=(duos // per_step,),
            in_specs=[
                pl.BlockSpec((per_step, edge, 2 * edge), block),
                pl.BlockSpec(incoming.shape, lambda g, *_: (0, 0, 0)),
                pl.BlockSpec((rows, hubs), whole),
                pl.BlockSpec((rows, edge), whole),
            ],
            out_specs=pl.BlockSpec((rows, edge), whole),
            scratch_shapes=[pltpu.VMEM((rows, edge), F32)],
        ),
        compiler_params=params(40, 1),
    )(row, owner_a, owner_b, n_duos, pairs, incoming, panel, inv)


def middle_kernel(
    feat, feat_peer, agg, agg_peer, cot, cot_peer, inv, panel, own_w, nbr_w,
    layer, slopes_out, agg_slopes_out, extra, hub_acc,
):
    step, steps = pl.program_id(0), pl.num_programs(0)
    half = feat.shape[1]
    preact = dot(jnp.concatenate([feat[...], feat_peer[...]], axis=1), own_w[...], NN) + dot(
        jnp.concatenate([agg[...], agg_peer[...]], axis=1), nbr_w[...], NN
    )
    layer[...] = jnp.maximum(preact[:, :half], 0.0).astype(BF16)
    cotangent = jnp.concatenate([cot[...], cot_peer[...]], axis=1).astype(F32)
    slopes = jnp.where(preact > 0, cotangent, 0.0).astype(BF16)
    slopes_out[...] = slopes
    agg_slopes = (dot(slopes, nbr_w[:half, :], NT) * inv[...]).astype(BF16)
    agg_slopes_out[...] = agg_slopes
    hub = dot(panel[...], agg_slopes, TN)

    @pl.when(step == 0)
    def _():
        hub_acc[...] = hub

    @pl.when(step > 0)
    def _():
        hub_acc[...] += hub

    @pl.when(step == steps - 1)
    def _():
        owners = hub_acc.shape[0] // 2
        extra[...] = jnp.zeros_like(extra)
        for j in range(2):
            extra[pl.ds(j, owners, stride=8), :] = hub_acc[pl.ds(j, owners, stride=2), :]


def middle(feat, feat_peer, agg, agg_peer, cot, cot_peer, inv, panel, own_w, nbr_w):
    rows, half = feat.shape
    hubs = panel.shape[1]
    block = 512
    by_row = lambda width: pl.BlockSpec((block, width), lambda g: (g, 0))
    whole = lambda shape: pl.BlockSpec(shape, lambda g: (0, 0))
    return pl.pallas_call(
        middle_kernel,
        name="middle",
        out_shape=(
            jax.ShapeDtypeStruct((rows, half), BF16),
            jax.ShapeDtypeStruct((rows, 2 * half), BF16),
            jax.ShapeDtypeStruct((rows, half), BF16),
            jax.ShapeDtypeStruct((4 * hubs, half), F32),
        ),
        grid=(rows // block,),
        in_specs=[by_row(half)] * 7
        + [by_row(hubs), whole(own_w.shape), whole(nbr_w.shape)],
        out_specs=(by_row(half), by_row(2 * half), by_row(half), whole((4 * hubs, half))),
        scratch_shapes=[pltpu.VMEM((hubs, half), F32)],
        compiler_params=params(32, 1),
    )(feat, feat_peer, agg, agg_peer, cot, cot_peer, inv, panel, own_w, nbr_w)


def back_kernel(order_row, order_owner, same, live, count, flipped, slopes, extra, out, carry):
    step = pl.program_id(0)
    slots, edge, _ = flipped.shape

    @pl.when(step == 0)
    def _():
        out[:, :edge, :] = jnp.zeros((out.shape[0], edge, out.shape[2]), out.dtype)
        out[:, edge:, :] = extra[...].astype(BF16)
        carry[...] = jnp.zeros_like(carry)

    @pl.when(step * slots < count[0])
    def _():
        products = []
        for i in range(slots):
            start = pl.multiple_of(order_row[step * slots + i] * edge, edge)
            products.append(dot(flipped[i], slopes[pl.ds(start, edge), :], NN))
        total = carry[...]
        for i in range(slots):
            k = step * slots + i
            total = products[i] * live[k].astype(F32) + total * same[k].astype(F32)
            out[order_owner[k], :edge, :] = total.astype(BF16)
        carry[...] = total


def back(order_row, order_owner, same, live, count, flipped, slopes, extra):
    slots, edge, _ = flipped.shape
    rows, half = slopes.shape
    parts = extra.shape[0]
    per_step = 16

    def block(g, order_row, order_owner, same, live, count):
        return (jnp.minimum(g, (count[0] - 1) // per_step), 0, 0)

    return pl.pallas_call(
        back_kernel,
        name="back",
        out_shape=jax.ShapeDtypeStruct((parts, edge + 8, half), BF16),
        grid_spec=pltpu.PrefetchScalarGridSpec(
            num_scalar_prefetch=5,
            grid=(slots // per_step,),
            in_specs=[
                pl.BlockSpec((per_step, edge, edge), block),
                pl.BlockSpec((rows, half), lambda g, *_: (0, 0)),
                pl.BlockSpec(extra.shape, lambda g, *_: (0, 0, 0)),
            ],
            out_specs=pl.BlockSpec((parts, edge + 8, half), lambda g, *_: (0, 0, 0)),
            scratch_shapes=[pltpu.VMEM((edge, half), F32)],
        ),
        compiler_params=params(58, 1),
    )(order_row, order_owner, same, live, count, flipped, slopes, extra)


def side_kernel(place, feat, agg, slopes, own_w, grads, direct, acc):
    step, steps = pl.program_id(0), pl.num_programs(0)
    half = feat.shape[1]
    s = slopes[...]
    direct[...] = dot(s, own_w[...], NT)
    part = dot(jnp.concatenate([feat[...], agg[...]], axis=1), s, TN)

    @pl.when(step == 0)
    def _():
        acc[...] = part

    @pl.when(step > 0)
    def _():
        acc[...] += part

    @pl.when(step == steps - 1)
    def _():
        n = half // 4
        for c in range(4):
            for r in range(4):
                grads[(c + 4 - place[0]) % 4, (r + 4 - place[1]) % 4] = acc[
                    (c // 2) * half + r * n : (c // 2) * half + (r + 1) * n,
                    (c % 2) * half : (c % 2 + 1) * half,
                ]


def side(place, feat, agg, slopes, own_w):
    rows, half = feat.shape
    block = 512
    by_row = lambda width: pl.BlockSpec((block, width), lambda g, *_: (g, 0))
    return pl.pallas_call(
        side_kernel,
        name="side",
        out_shape=(
            jax.ShapeDtypeStruct((4, 4, half // 4, half), F32),
            jax.ShapeDtypeStruct((rows, half), F32),
        ),
        grid_spec=pltpu.PrefetchScalarGridSpec(
            num_scalar_prefetch=1,
            grid=(rows // block,),
            in_specs=[
                by_row(half),
                by_row(half),
                by_row(2 * half),
                pl.BlockSpec(own_w.shape, lambda g, *_: (0, 0)),
            ],
            out_specs=(
                pl.BlockSpec((4, 4, half // 4, half), lambda g, *_: (0, 0, 0, 0)),
                by_row(half),
            ),
            scratch_shapes=[pltpu.VMEM((2 * half, 2 * half), F32)],
        ),
        compiler_params=params(24, 1),
    )(place, feat, agg, slopes, own_w)


def finish_kernel(send, hubs, returned, direct, out, total):
    step, steps = pl.program_id(0), pl.num_programs(0)
    parts, height, half = returned.shape
    edge = out.shape[1]

    @pl.when(step == 0)
    def _():
        out[...] = direct[...]
        total[...] = jnp.zeros_like(total)

    share = total[...]
    for i in range(parts):
        out[send[step * parts + i]] += returned[i, :edge, :].astype(F32)
        share = share + returned[i, edge:, :].astype(F32)
    total[...] = share

    @pl.when(step == steps - 1)
    def _():
        for j in range(2):
            row = hubs[j]
            tile, inside = row // edge, row % edge
            base = pl.multiple_of((inside // 8) * 8, 8)
            here = lax.broadcasted_iota(jnp.int32, (8, half), 0) == inside - base
            out[tile, pl.ds(base, 8), :] += jnp.where(here, total[j : j + 1, :], 0.0)


def finish(send_tile, hub_rows, returned, direct):
    tiles, edge, half = direct.shape
    parts, height, _ = returned.shape
    per_step = 16
    whole = pl.BlockSpec((tiles, edge, half), lambda g, *_: (0, 0, 0))
    return pl.pallas_call(
        finish_kernel,
        name="finish",
        out_shape=jax.ShapeDtypeStruct(direct.shape, F32),
        grid_spec=pltpu.PrefetchScalarGridSpec(
            num_scalar_prefetch=2,
            grid=(parts // per_step,),
            in_specs=[
                pl.BlockSpec((per_step, height, half), lambda g, *_: (g, 0, 0)),
                whole,
            ],
            out_specs=whole,
            scratch_shapes=[pltpu.VMEM((8, half), F32)],
        ),
        compiler_params=params(24, 1),
    )(send_tile, hub_rows, returned, direct)


def plan(tile_row, tile_owner, tile_count, tiles, parts):
    slots = tile_row.shape[0]
    index = jnp.arange(slots, dtype=jnp.int32)
    live = index < tile_count[0]
    earlier = index[None, :] < index[:, None]
    pick = lambda where, what: jnp.sum(jnp.where(where, what, 0), axis=1, dtype=jnp.int32)

    key = jnp.where(live, tile_owner, parts)
    before = (key[None, :] < key[:, None]) | ((key[None, :] == key[:, None]) & earlier)
    rank = jnp.sum(before, axis=1, dtype=jnp.int32)
    last = jnp.minimum(index, tile_count[0] - 1)
    at = rank[None, :] == last[:, None]
    order = pick(at, index[None, :])
    order_row = pick(at, tile_row[None, :])
    order_owner = pick(at, tile_owner[None, :])
    same = jnp.concatenate([jnp.zeros((1,), jnp.int32), (order_owner[1:] == order_owner[:-1]).astype(jnp.int32)])
    live_int = live.astype(jnp.int32)

    mates = live[None, :] & (tile_row[None, :] == tile_row[:, None])
    inside = jnp.sum(mates & earlier, axis=1, dtype=jnp.int32)
    rows = jnp.arange(tiles, dtype=jnp.int32)
    per_row = jnp.sum(live[None, :] & (tile_row[None, :] == rows[:, None]), axis=1, dtype=jnp.int32)
    row_pairs = (per_row + 1) // 2
    lower = jnp.sum(
        jnp.where(rows[None, :] < tile_row[:, None], row_pairs[None, :], 0), axis=1, dtype=jnp.int32
    )
    pair = jnp.where(live, lower + inside // 2, -1)
    duos = (slots + tiles) // 2
    p = jnp.arange(duos, dtype=jnp.int32)
    is_first = (pair[None, :] == p[:, None]) & (inside[None, :] % 2 == 0)
    is_second = (pair[None, :] == p[:, None]) & (inside[None, :] % 2 == 1)
    first = pick(is_first, index[None, :])
    second = pick(is_second, index[None, :])
    owner_a = pick(is_first, tile_owner[None, :])
    owner_b = pick(is_second, tile_owner[None, :])
    pair_row = pick(is_first, tile_row[None, :])
    kinds = pick(is_first, 1) + pick(is_second, 1)
    n_duos = jnp.sum(row_pairs, dtype=jnp.int32).reshape(1)
    return (
        (order, order_row, order_owner, same, live_int),
        (first, second, kinds, pair_row, owner_a, owner_b, n_duos),
        duos,
    )


def exchange(block):
    return lax.all_to_all(block, "dom", split_axis=0, concat_axis=0, tiled=True)


def swap(block):
    return lax.ppermute(block, "feat", [(0, 1), (1, 0)])


def move(block, axis, amount):
    def target(d):
        z, x, y = d // 16, (d // 4) % 4, d % 4
        if axis == "y":
            y = (y + amount) % 4
        elif axis == "x":
            x = (x + amount) % 4
        else:
            z = z ^ amount
        return (z * 4 + x) * 4 + y

    return lax.ppermute(block, "dom", [(d, target(d)) for d in range(lax.axis_size("dom"))])


def sum_over_dom(blocks):
    for axis in ("y", "x"):
        moved = [move(blocks[i], axis, i) for i in (1, 2, 3)]
        blocks = (blocks[0] + moved[0]) + (moved[1] + moved[2])
    for bit in (1, 2, 4):
        blocks = blocks + move(blocks, "z", bit)
    for axis in ("x", "y"):
        blocks = jnp.stack([blocks] + [move(blocks, axis, i) for i in (1, 2, 3)])
    return blocks


def shards(
    features,
    self_weight,
    neighbor_weight,
    tile_values,
    tile_row,
    tile_owner,
    send_tile,
    tile_count,
    hub_panel,
    hub_rows,
    cotangent,
):
    rows_dev, half = features.shape
    tile_edge = tile_values.shape[1]
    tiles_dev = rows_dev // tile_edge
    dom_size = lax.axis_size("dom")
    core = lax.axis_index("feat")

    outgoing = pack(features, send_tile, hub_rows, tile_edge)
    incoming = exchange(outgoing)

    def own_first(w):
        return jnp.where(core == 0, w, jnp.concatenate([w[:, half:], w[:, :half]], axis=1))

    weights = own_first(jnp.concatenate([self_weight, neighbor_weight], axis=0))
    peer_weights = swap(weights)
    peer_weights = jnp.concatenate([peer_weights[:, half:], peer_weights[:, :half]], axis=1)
    own_w = jnp.concatenate([weights[:half], peer_weights[:half]], axis=0)
    nbr_w = jnp.concatenate([weights[half:], peer_weights[half:]], axis=0)
    feat_peer = swap(features)
    cot_peer = swap(cotangent)

    by_owner, by_row, duos = plan(tile_row, tile_owner, tile_count, tiles_dev, dom_size)
    order, order_row, order_owner, same, live = by_owner
    first, second, kinds, pair_row, owner_a, owner_b, n_duos = by_row
    tile_count, own_w, nbr_w, feat_peer, cot_peer = lax.optimization_barrier(
        (tile_count, own_w, nbr_w, feat_peer, cot_peer)
    )
    inv, flipped, pairs = prepare(
        tile_row, tile_count, order, first, second, kinds, tile_values, hub_panel, duos
    )

    aggregate = gather(pair_row, owner_a, owner_b, n_duos, pairs, incoming, hub_panel, inv)
    agg_peer = swap(aggregate)
    layer_out, slopes, agg_slopes, extra = middle(
        features, feat_peer, aggregate, agg_peer, cotangent, cot_peer, inv, hub_panel, own_w, nbr_w
    )
    terms = back(
        order_row, order_owner, same, live, tile_count, flipped, agg_slopes,
        extra.reshape(dom_size, 8, half),
    )
    returned = exchange(terms)

    _, slopes = lax.optimization_barrier((terms, slopes))
    dom = lax.axis_index("dom")
    place_y, place_x = dom % 4, (dom // 4) % 4
    grads, direct = side(
        jnp.stack([place_y, place_x]).astype(jnp.int32), features, aggregate, slopes, own_w[:half]
    )
    grads = sum_over_dom(grads)
    c = jnp.arange(4) ^ core
    r = jnp.arange(4)
    index = (((place_y - c) % 4)[:, None] * 4 + ((place_x - r) % 4)[None, :]).reshape(16)
    grads = grads.reshape(16, half // 4, half)[index].reshape(4, half, half)
    grads = grads * (1.0 / math.sqrt(rows_dev * dom_size))
    self_grad = jnp.concatenate([grads[0], grads[1]], axis=1)
    neighbor_grad = jnp.concatenate([grads[2], grads[3]], axis=1)
    direct = direct.reshape(tiles_dev, tile_edge, half)
    direct, self_grad, neighbor_grad = lax.optimization_barrier((direct, self_grad, neighbor_grad))
    input_grad = finish(send_tile, hub_rows, returned, direct).reshape(rows_dev, half)
    return (layer_out, self_grad, neighbor_grad, input_grad)


def solution(mesh):
    placed = (
        P("dom", "feat"),
        P("feat", None),
        P("feat", None),
        P("dom", None, None),
        P("dom"),
        P("dom"),
        P("dom"),
        P("dom"),
        P("dom", None),
        P("dom"),
        P("dom", "feat"),
    )
    return jax.shard_map(
        shards,
        mesh=mesh,
        in_specs=placed,
        out_specs=(P("dom", "feat"), P("feat", None), P("feat", None), P("dom", "feat")),
        check_vma=False,
    )
```

```python
import math

import jax
import jax.numpy as jnp
from jax import lax
from jax.experimental import pallas as pl
from jax.experimental.pallas import tpu as pltpu
from jax.sharding import PartitionSpec as P

F32 = jnp.float32
BF16 = jnp.bfloat16
MIB = 1 << 20


def dot(a, b, dims):
    return lax.dot_general(a, b, (dims, ((), ())), preferred_element_type=F32)


NN = ((1,), (0,))
NT = ((1,), (1,))
TN = ((0,), (0,))


def params(mib, steps):
    return pltpu.CompilerParams(
        dimension_semantics=("arbitrary",) * steps, vmem_limit_bytes=mib * MIB
    )


ANY = pl.BlockSpec(memory_space=pl.ANY)
HBM = pl.BlockSpec(memory_space=pltpu.HBM)


def own_copies(mib):
    return pltpu.CompilerParams(vmem_limit_bytes=mib * MIB)


def pack_kernel(send, hubs, feat, out, hub_rows, tails, sems):
    parts, height, width = out.shape
    edge = height - 8

    @pl.loop(0, parts // 8)
    def _(g):
        for i in range(8):
            q = g * 8 + i
            start = pl.multiple_of(send[q] * edge, edge)
            pltpu.make_async_copy(
                feat.at[pl.ds(start, edge), :], out.at[q, pl.ds(0, edge), :], sems.at[0]
            ).start()

    hub_rows[...] = jnp.zeros_like(hub_rows)
    for j in range(2):
        row = hubs[j]
        base = pl.multiple_of((row // 16) * 16, 16)
        block = feat[pl.ds(base, 16), :].astype(F32)
        here = lax.broadcasted_iota(jnp.int32, block.shape, 0) == row - base
        hub_rows[j : j + 1, :] = jnp.sum(jnp.where(here, block, 0.0), axis=0, keepdims=True)
    tails[...] = jnp.broadcast_to(hub_rows[...].astype(BF16)[None], tails.shape)
    tail = out.at[:, pl.ds(edge, 8), :]
    pltpu.make_async_copy(tails, tail, sems.at[1]).start()
    pltpu.make_async_copy(tails, tail, sems.at[1]).wait()
    body = out.at[:, pl.ds(0, edge), :]
    pltpu.make_async_copy(body, body, sems.at[0]).wait()


def pack(features, send_tile, hub_rows, edge):
    rows, width = features.shape
    parts = send_tile.shape[0]
    return pl.pallas_call(
        pack_kernel,
        name="pack",
        out_shape=jax.ShapeDtypeStruct((parts, edge + 8, width), BF16),
        grid_spec=pltpu.PrefetchScalarGridSpec(
            num_scalar_prefetch=2,
            grid=(1,),
            in_specs=[pl.BlockSpec((rows, width), lambda g, *_: (0, 0))],
            out_specs=HBM,
            scratch_shapes=[
                pltpu.VMEM((8, width), F32),
                pltpu.VMEM((parts, 8, width), BF16),
                pltpu.SemaphoreType.DMA((2,)),
            ],
        ),
        compiler_params=own_copies(58),
    )(send_tile, hub_rows, features)


def prepare_kernel(
    row, count, order, first, second, kinds, values, panel, *rest
):
    inv, flipped, pairs, squares = rest[-4:]
    step, steps = pl.program_id(0), pl.num_programs(0)
    edge = values.shape[1]
    slots, duos = flipped.shape[0], pairs.shape[0]

    @pl.when(step == 0)
    def _():
        squares[...] = jnp.zeros_like(squares)

    @pl.loop(0, slots)
    def _(i):
        k = step * slots + i
        flipped[i] = values[order[k]].T
        tile = values[k].astype(F32)
        live = (k < count[0]).astype(F32)
        start = pl.multiple_of(row[k] * edge, edge)
        squares[pl.ds(start, edge), :] += tile * tile * live

    @pl.loop(0, duos)
    def _(i):
        p = step * duos + i
        has_first = (kinds[p] > 0).astype(BF16)
        has_second = (kinds[p] > 1).astype(BF16)
        pairs[i, :, :edge] = values[first[p]] * has_first
        pairs[i, :, edge:] = values[second[p]] * has_second

    @pl.when(step == steps - 1)
    def _():
        @pl.loop(0, squares.shape[0] // edge)
        def _(t):
            at = pl.ds(pl.multiple_of(t * edge, edge), edge)
            wide = panel[at, :].astype(F32)
            wide = wide * wide
            half = wide.shape[1] // 2
            total = jnp.sum(
                squares[at, :] + wide[:, :half] + wide[:, half:], axis=1, keepdims=True
            )
            inv[at, :] = jnp.broadcast_to(lax.rsqrt(1.0 + total), (edge, inv.shape[1]))


def prepare(row, count, order, first, second, kinds, values, panel, duos, ready):
    slots, edge, _ = values.shape
    rows, hubs = panel.shape
    steps = 4
    whole = lambda g, *_: (0, 0)
    return pl.pallas_call(
        prepare_kernel,
        name="prepare",
        out_shape=(
            jax.ShapeDtypeStruct((rows, edge), F32),
            jax.ShapeDtypeStruct((slots, edge, edge), BF16),
            jax.ShapeDtypeStruct((duos, edge, 2 * edge), BF16),
        ),
        grid_spec=pltpu.PrefetchScalarGridSpec(
            num_scalar_prefetch=6,
            grid=(steps,),
            in_specs=[
                pl.BlockSpec((slots, edge, edge), lambda g, *_: (0, 0, 0)),
                pl.BlockSpec((rows, hubs), whole),
            ]
            + [ANY] * len(ready),
            out_specs=(
                pl.BlockSpec((rows, edge), whole),
                pl.BlockSpec((slots // steps, edge, edge), lambda g, *_: (g, 0, 0)),
                pl.BlockSpec((duos // steps, edge, 2 * edge), lambda g, *_: (g, 0, 0)),
            ),
            scratch_shapes=[pltpu.VMEM((rows, edge), F32)],
        ),
        compiler_params=params(40, 1),
        cost_estimate=pl.CostEstimate(
            flops=60_000_000_000, bytes_accessed=40_000_000, transcendentals=0
        ),
    )(row, count, order, first, second, kinds, values, panel, *ready)


DUO_STEP = 16


def gather_kernel(
    row, owner_a, owner_b, n_duos, pairs, incoming, panel, inv, out,
    tail, pan, tiles, norm, duos, tail_wide, hub_wide, sums, result, sems, duo_sems, out_sems,
):
    parts, edge, _ = tiles.shape
    rows = sums.shape[0]
    copy = pltpu.make_async_copy
    tail_in = copy(incoming.at[:, pl.ds(edge, 8), :], tail, sems.at[0])
    panel_in = copy(panel, pan, sems.at[1])
    tiles_in = copy(incoming.at[:, pl.ds(0, edge), :], tiles, sems.at[2])
    norm_in = copy(inv, norm, sems.at[3])
    steps = duos.shape[0] // DUO_STEP
    duo_in = [
        copy(pairs.at[pl.ds(c * DUO_STEP, DUO_STEP)], duos.at[pl.ds(c * DUO_STEP, DUO_STEP)], duo_sems.at[c])
        for c in range(steps)
    ]
    tail_in.start()
    panel_in.start()
    tiles_in.start()
    for c in range(steps):

        @pl.when(c * DUO_STEP < n_duos[0])
        def _():
            duo_in[c].start()

    norm_in.start()

    tail_in.wait()
    tail_wide[...] = tail[...].reshape(tail_wide.shape).astype(F32)
    for j in range(2):
        hub_wide[pl.ds(j, parts, stride=2), :] = tail_wide[pl.ds(j, parts, stride=8), :]
    hub_feats = hub_wide[...].astype(BF16)
    panel_in.wait()
    block = 512
    for t in range(rows // block):
        at = pl.ds(t * block, block)
        sums[at, :] = dot(pan[at, :], hub_feats, NN)
    tiles_in.wait()
    for c in range(steps):

        @pl.when(c * DUO_STEP < n_duos[0])
        def _():
            duo_in[c].wait()
            products = []
            for i in range(DUO_STEP):
                p = c * DUO_STEP + i
                columns = jnp.concatenate([tiles[owner_a[p]], tiles[owner_b[p]]], axis=0)
                products.append(dot(duos[p], columns, NN))
            for i in range(DUO_STEP):
                start = pl.multiple_of(row[c * DUO_STEP + i] * edge, edge)
                sums[pl.ds(start, edge), :] += products[i]

    norm_in.wait()
    block = rows // 4
    sent = []
    for t in range(4):
        at = pl.ds(t * block, block)
        result[at, :] = (sums[at, :] * norm[at, :]).astype(BF16)
        sent.append(copy(result.at[at, :], out.at[at, :], out_sems.at[t]))
        sent[-1].start()
    for s in sent:
        s.wait()


def gather(row, owner_a, owner_b, n_duos, pairs, incoming, panel, inv):
    duos, edge, _ = pairs.shape
    rows, hubs = panel.shape
    parts = incoming.shape[0]
    return pl.pallas_call(
        gather_kernel,
        name="gather",
        out_shape=jax.ShapeDtypeStruct((rows, edge), BF16),
        grid_spec=pltpu.PrefetchScalarGridSpec(
            num_scalar_prefetch=4,
            grid=(1,),
            in_specs=[ANY] * 4,
            out_specs=HBM,
            scratch_shapes=[
                pltpu.VMEM((parts, 8, edge), BF16),
                pltpu.VMEM((rows, hubs), BF16),
                pltpu.VMEM((parts, edge, edge), BF16),
                pltpu.VMEM((rows, edge), F32),
                pltpu.VMEM(pairs.shape, BF16),
                pltpu.VMEM((parts * 8, edge), F32),
                pltpu.VMEM((hubs, edge), F32),
                pltpu.VMEM((rows, edge), F32),
                pltpu.VMEM((rows, edge), BF16),
                pltpu.SemaphoreType.DMA((4,)),
                pltpu.SemaphoreType.DMA((duos // DUO_STEP,)),
                pltpu.SemaphoreType.DMA((4,)),
            ],
        ),
        compiler_params=own_copies(58),
    )(row, owner_a, owner_b, n_duos, pairs, incoming, panel, inv)


ROW_STEPS = 4
MID_MIB = 56
SLOT_STEP = 16


def middle_kernel(
    order_row, order_owner, count,
    feat, feat_peer, agg, agg_peer, cot, cot_peer, inv, panel, flipped, own_w, nbr_w,
    layer, slopes, terms,
    feat_v, feat_peer_v, agg_v, agg_peer_v, cot_v, cot_peer_v, inv_v, panel_v, flipped_v,
    layer_v, slopes_v, agg_slopes, terms_v, hub_acc, hub_wide, carry,
    in_sems, flip_sems, out_sems, term_sems,
):
    rows, half = feat_v.shape
    slots, edge, _ = flipped_v.shape
    parts = terms_v.shape[0]
    copy = pltpu.make_async_copy
    block = rows // ROW_STEPS
    sources = (feat, feat_peer, agg, agg_peer, cot, cot_peer, inv, panel)
    places = (feat_v, feat_peer_v, agg_v, agg_peer_v, cot_v, cot_peer_v, inv_v, panel_v)
    at = [pl.ds(t * block, block) for t in range(ROW_STEPS)]
    inputs = [
        [copy(s.at[at[t], :], d.at[at[t], :], in_sems.at[t, i]) for i, (s, d) in enumerate(zip(sources, places))]
        for t in range(ROW_STEPS)
    ]
    steps = slots // SLOT_STEP
    flips = [
        copy(flipped.at[pl.ds(b * SLOT_STEP, SLOT_STEP)], flipped_v.at[pl.ds(b * SLOT_STEP, SLOT_STEP)], flip_sems.at[b])
        for b in range(steps)
    ]
    for t in range(ROW_STEPS):
        for c in inputs[t]:
            c.start()
    for b in range(steps):

        @pl.when(b * SLOT_STEP < count[0])
        def _():
            flips[b].start()

    terms_v[:, :edge, :] = jnp.zeros((parts, edge, half), BF16)
    hub_wide[...] = jnp.zeros_like(hub_wide)
    carry[...] = jnp.zeros_like(carry)

    sent = []
    for t in range(ROW_STEPS):
        for c in inputs[t]:
            c.wait()
        here = at[t]
        preact = dot(
            jnp.concatenate([feat_v[here, :], feat_peer_v[here, :]], axis=1), own_w[...], NN
        ) + dot(jnp.concatenate([agg_v[here, :], agg_peer_v[here, :]], axis=1), nbr_w[...], NN)
        layer_v[here, :] = jnp.maximum(preact[:, :half], 0.0).astype(BF16)
        cotangent = jnp.concatenate([cot_v[here, :], cot_peer_v[here, :]], axis=1).astype(F32)
        slope = jnp.where(preact > 0, cotangent, 0.0).astype(BF16)
        slopes_v[here, :] = slope
        sent.append(copy(layer_v.at[here, :], layer.at[here, :], out_sems.at[t, 0]))
        sent.append(copy(slopes_v.at[here, :], slopes.at[here, :], out_sems.at[t, 1]))
        sent[-2].start()
        sent[-1].start()
        back = (dot(slope, nbr_w[:half, :], NT) * inv_v[here, :]).astype(BF16)
        agg_slopes[here, :] = back
        hub = dot(panel_v[here, :], back, TN)
        if t == 0:
            hub_acc[...] = hub
        else:
            hub_acc[...] += hub

    for j in range(2):
        hub_wide[pl.ds(j, parts, stride=8), :] = hub_acc[pl.ds(j, parts, stride=2), :]
    terms_v[:, edge:, :] = hub_wide[...].reshape(parts, 8, half).astype(BF16)

    group = parts // 8
    for b in range(steps):

        @pl.when(b * SLOT_STEP < count[0])
        def _():
            flips[b].wait()
            products = []
            for i in range(SLOT_STEP):
                k = b * SLOT_STEP + i
                start = pl.multiple_of(order_row[k] * edge, edge)
                products.append(dot(flipped_v[k], agg_slopes[pl.ds(start, edge), :], NN))
            total = carry[...]
            for i in range(SLOT_STEP):
                k = b * SLOT_STEP + i
                live = (k < count[0]).astype(F32)
                fresh = products[i] * live
                if k:
                    same = (order_owner[k] == order_owner[k - 1]).astype(F32)
                    total = fresh + total * same
                else:
                    total = fresh
                terms_v[order_owner[k], :edge, :] = total.astype(BF16)
            carry[...] = total
            first = order_owner[b * SLOT_STEP] // group if b else 0
            after = (b + 1) * SLOT_STEP
            last = jnp.where(
                after >= count[0], parts // group, order_owner[min(after, slots - 1)] // group
            )

            @pl.loop(first, last)
            def _(g):
                owners = pl.ds(g * group, group)
                copy(terms_v.at[owners], terms.at[owners], term_sems.at[0]).start()

    for c in sent:
        c.wait()
    copy(terms_v, terms, term_sems.at[0]).wait()


def middle(
    order_row, order_owner, count,
    feat, feat_peer, agg, agg_peer, cot, cot_peer, inv, panel, flipped, own_w, nbr_w, parts,
):
    rows, half = feat.shape
    hubs = panel.shape[1]
    edge = flipped.shape[1]
    narrow = pltpu.VMEM((rows, half), BF16)
    wide = pltpu.VMEM((rows, 2 * half), BF16)
    whole = lambda g, *_: (0, 0)
    height = edge + 8
    return pl.pallas_call(
        middle_kernel,
        name="middle",
        out_shape=(
            jax.ShapeDtypeStruct((rows, half), BF16),
            jax.ShapeDtypeStruct((rows, 2 * half), BF16),
            jax.ShapeDtypeStruct((parts, height, half), BF16),
        ),
        grid_spec=pltpu.PrefetchScalarGridSpec(
            num_scalar_prefetch=3,
            grid=(1,),
            in_specs=[ANY] * 9
            + [pl.BlockSpec(own_w.shape, whole), pl.BlockSpec(nbr_w.shape, whole)],
            out_specs=(HBM, HBM, HBM),
            scratch_shapes=[narrow] * 6
            + [
                pltpu.VMEM((rows, half), F32),
                pltpu.VMEM((rows, hubs), BF16),
                pltpu.VMEM(flipped.shape, BF16),
                narrow,
                wide,
                narrow,
                pltpu.VMEM((parts, height, half), BF16),
                pltpu.VMEM((hubs, half), F32),
                pltpu.VMEM((4 * hubs, half), F32),
                pltpu.VMEM((edge, half), F32),
                pltpu.SemaphoreType.DMA((ROW_STEPS, 8)),
                pltpu.SemaphoreType.DMA((flipped.shape[0] // SLOT_STEP,)),
                pltpu.SemaphoreType.DMA((ROW_STEPS, 2)),
                pltpu.SemaphoreType.DMA((1,)),
            ],
        ),
        compiler_params=own_copies(MID_MIB),
    )(
        order_row, order_owner, count,
        feat, feat_peer, agg, agg_peer, cot, cot_peer, inv, panel, flipped, own_w, nbr_w,
    )


def side_kernel(place, feat, agg, slopes, own_w, grads, direct, acc):
    step, steps = pl.program_id(0), pl.num_programs(0)
    half = feat.shape[1]
    s = slopes[...]
    direct[...] = dot(s, own_w[...], NT)
    part = dot(jnp.concatenate([feat[...], agg[...]], axis=1), s, TN)

    @pl.when(step == 0)
    def _():
        acc[...] = part

    @pl.when(step > 0)
    def _():
        acc[...] += part

    @pl.when(step == steps - 1)
    def _():
        n = half // 4
        for c in range(4):
            for r in range(4):
                grads[(c + 4 - place[0]) % 4, (r + 4 - place[1]) % 4] = acc[
                    (c // 2) * half + r * n : (c // 2) * half + (r + 1) * n,
                    (c % 2) * half : (c % 2 + 1) * half,
                ]


def side(place, feat, agg, slopes, own_w):
    rows, half = feat.shape
    block = 512
    by_row = lambda width: pl.BlockSpec((block, width), lambda g, *_: (g, 0))
    return pl.pallas_call(
        side_kernel,
        name="side",
        out_shape=(
            jax.ShapeDtypeStruct((4, 4, half // 4, half), F32),
            jax.ShapeDtypeStruct((rows, half), F32),
        ),
        grid_spec=pltpu.PrefetchScalarGridSpec(
            num_scalar_prefetch=1,
            grid=(rows // block,),
            in_specs=[
                by_row(half),
                by_row(half),
                by_row(2 * half),
                pl.BlockSpec(own_w.shape, lambda g, *_: (0, 0)),
            ],
            out_specs=(
                pl.BlockSpec((4, 4, half // 4, half), lambda g, *_: (0, 0, 0, 0)),
                by_row(half),
            ),
            scratch_shapes=[pltpu.VMEM((2 * half, 2 * half), F32)],
        ),
        compiler_params=params(24, 1),
    )(place, feat, agg, slopes, own_w)


def finish_kernel(send, hubs, returned, direct, grads, out, grads_out, acc, landed, sems, part_sems):
    parts, height, half = landed.shape
    edge = acc.shape[1]
    copy = pltpu.make_async_copy
    steps = 8
    group = parts // steps
    arrivals = [
        copy(returned.at[pl.ds(g * group, group)], landed.at[pl.ds(g * group, group)], part_sems.at[g])
        for g in range(steps)
    ]
    start = copy(direct, acc, sems.at[0])
    start.start()
    grads_out[...] = grads[...]
    for c in arrivals:
        c.start()
    start.wait()
    total = jnp.zeros((8, half), F32)
    for g in range(steps):
        arrivals[g].wait()
        for i in range(group):
            p = g * group + i
            acc[send[p]] += landed[p, :edge, :].astype(F32)
            total = total + landed[p, edge:, :].astype(F32)
    for j in range(2):
        row = hubs[j]
        tile, inside = row // edge, row % edge
        base = pl.multiple_of((inside // 8) * 8, 8)
        here = lax.broadcasted_iota(jnp.int32, (8, half), 0) == inside - base
        acc[tile, pl.ds(base, 8), :] += jnp.where(here, total[j : j + 1, :], 0.0)
    end = copy(acc, out, sems.at[1])
    end.start()
    end.wait()


def finish(send_tile, hub_rows, returned, direct, grads):
    small = pl.BlockSpec(grads.shape, lambda g, *_: (0, 0))
    return pl.pallas_call(
        finish_kernel,
        name="finish",
        out_shape=(
            jax.ShapeDtypeStruct(direct.shape, F32),
            jax.ShapeDtypeStruct(grads.shape, F32),
        ),
        grid_spec=pltpu.PrefetchScalarGridSpec(
            num_scalar_prefetch=2,
            grid=(1,),
            in_specs=[ANY, ANY, small],
            out_specs=(HBM, small),
            scratch_shapes=[
                pltpu.VMEM(direct.shape, F32),
                pltpu.VMEM(returned.shape, BF16),
                pltpu.SemaphoreType.DMA((2,)),
                pltpu.SemaphoreType.DMA((8,)),
            ],
        ),
        compiler_params=own_copies(58),
    )(send_tile, hub_rows, returned, direct, grads)


def plan(tile_row, tile_owner, tile_count, tiles, parts):
    slots = tile_row.shape[0]
    index = jnp.arange(slots, dtype=jnp.int32)
    live = index < tile_count[0]
    earlier = index[None, :] < index[:, None]
    pick = lambda where, what: jnp.sum(jnp.where(where, what, 0), axis=1, dtype=jnp.int32)

    key = jnp.where(live, tile_owner, parts)
    before = (key[None, :] < key[:, None]) | ((key[None, :] == key[:, None]) & earlier)
    rank = jnp.sum(before, axis=1, dtype=jnp.int32)
    last = jnp.minimum(index, tile_count[0] - 1)
    at = rank[None, :] == last[:, None]
    order = pick(at, index[None, :])
    order_row = pick(at, tile_row[None, :])
    order_owner = pick(at, tile_owner[None, :])

    mates = live[None, :] & (tile_row[None, :] == tile_row[:, None])
    inside = jnp.sum(mates & earlier, axis=1, dtype=jnp.int32)
    rows = jnp.arange(tiles, dtype=jnp.int32)
    per_row = jnp.sum(live[None, :] & (tile_row[None, :] == rows[:, None]), axis=1, dtype=jnp.int32)
    row_pairs = (per_row + 1) // 2
    lower = jnp.sum(
        jnp.where(rows[None, :] < tile_row[:, None], row_pairs[None, :], 0), axis=1, dtype=jnp.int32
    )
    pair = jnp.where(live, lower + inside // 2, -1)
    duos = (slots + tiles) // 2
    p = jnp.arange(duos, dtype=jnp.int32)
    is_first = (pair[None, :] == p[:, None]) & (inside[None, :] % 2 == 0)
    is_second = (pair[None, :] == p[:, None]) & (inside[None, :] % 2 == 1)
    first = pick(is_first, index[None, :])
    second = pick(is_second, index[None, :])
    owner_a = pick(is_first, tile_owner[None, :])
    owner_b = pick(is_second, tile_owner[None, :])
    pair_row = pick(is_first, tile_row[None, :])
    kinds = pick(is_first, 1) + pick(is_second, 1)
    n_duos = jnp.sum(row_pairs, dtype=jnp.int32).reshape(1)
    return (
        (order, order_row, order_owner),
        (first, second, kinds, pair_row, owner_a, owner_b, n_duos),
        duos,
    )


def exchange(block):
    return lax.all_to_all(block, "dom", split_axis=0, concat_axis=0, tiled=True)


def swap(block):
    return lax.ppermute(block, "feat", [(0, 1), (1, 0)])


def move(block, axis, amount):
    def target(d):
        z, x, y = d // 16, (d // 4) % 4, d % 4
        if axis == "y":
            y = (y + amount) % 4
        elif axis == "x":
            x = (x + amount) % 4
        else:
            z = z ^ amount
        return (z * 4 + x) * 4 + y

    return lax.ppermute(block, "dom", [(d, target(d)) for d in range(lax.axis_size("dom"))])


def add_up(blocks):
    for axis in ("y", "x"):
        moved = [move(blocks[i], axis, i) for i in (1, 2, 3)]
        blocks = (blocks[0] + moved[0]) + (moved[1] + moved[2])
    lines = [blocks] + [move(blocks, "z", bits) for bits in range(1, 8)]
    while len(lines) > 1:
        lines = [a + b for a, b in zip(lines[::2], lines[1::2])]
    return lines[0]


def shards(
    features,
    self_weight,
    neighbor_weight,
    tile_values,
    tile_row,
    tile_owner,
    send_tile,
    tile_count,
    hub_panel,
    hub_rows,
    cotangent,
):
    rows_dev, half = features.shape
    tile_edge = tile_values.shape[1]
    tiles_dev = rows_dev // tile_edge
    dom_size = lax.axis_size("dom")
    core = lax.axis_index("feat")

    outgoing = pack(features, send_tile, hub_rows, tile_edge)
    incoming = exchange(outgoing)

    def own_first(w):
        return jnp.where(core == 0, w, jnp.concatenate([w[:, half:], w[:, :half]], axis=1))

    weights = own_first(jnp.concatenate([self_weight, neighbor_weight], axis=0))
    peer_weights = swap(weights)
    peer_weights = jnp.concatenate([peer_weights[:, half:], peer_weights[:, :half]], axis=1)
    own_w = jnp.concatenate([weights[:half], peer_weights[:half]], axis=0)
    nbr_w = jnp.concatenate([weights[half:], peer_weights[half:]], axis=0)
    feat_peer = swap(features)
    cot_peer = swap(cotangent)

    by_owner, by_row, duos = plan(tile_row, tile_owner, tile_count, tiles_dev, dom_size)
    order, order_row, order_owner = by_owner
    first, second, kinds, pair_row, owner_a, owner_b, n_duos = by_row
    inv, flipped, pairs = prepare(
        tile_row, tile_count, order, first, second, kinds, tile_values, hub_panel, duos,
        (own_w, nbr_w, feat_peer, cot_peer),
    )

    aggregate = gather(pair_row, owner_a, owner_b, n_duos, pairs, incoming, hub_panel, inv)
    agg_peer = swap(aggregate)
    layer_out, slopes, terms = middle(
        order_row, order_owner, tile_count,
        features, feat_peer, aggregate, agg_peer, cotangent, cot_peer, inv, hub_panel, flipped,
        own_w, nbr_w, dom_size,
    )
    returned = exchange(terms)

    dom = lax.axis_index("dom")
    place_y, place_x = dom % 4, (dom // 4) % 4
    grads, direct = side(
        jnp.stack([place_y, place_x]).astype(jnp.int32), features, aggregate, slopes, own_w[:half]
    )
    grads = add_up(grads)
    from_x = [move(grads, "x", i) for i in (1, 2, 3)]
    input_grad, grads = finish(
        send_tile, hub_rows, returned, direct.reshape(tiles_dev, tile_edge, half), grads
    )
    input_grad = input_grad.reshape(rows_dev, half)
    grads = jnp.stack([grads] + from_x)
    grads = jnp.stack([grads] + [move(grads, "y", i) for i in (1, 2, 3)])
    c = jnp.arange(4) ^ core
    r = jnp.arange(4)
    index = (((place_y - c) % 4)[:, None] * 4 + ((place_x - r) % 4)[None, :]).reshape(16)
    grads = grads.reshape(16, half // 4, half)[index].reshape(4, half, half)
    grads = grads * (1.0 / math.sqrt(rows_dev * dom_size))
    self_grad = jnp.concatenate([grads[0], grads[1]], axis=1)
    neighbor_grad = jnp.concatenate([grads[2], grads[3]], axis=1)
    return (layer_out, self_grad, neighbor_grad, input_grad)


def solution(mesh):
    placed = (
        P("dom", "feat"),
        P("feat", None),
        P("feat", None),
        P("dom", None, None),
        P("dom"),
        P("dom"),
        P("dom"),
        P("dom"),
        P("dom", None),
        P("dom"),
        P("dom", "feat"),
    )
    return jax.shard_map(
        shards,
        mesh=mesh,
        in_specs=placed,
        out_specs=(P("dom", "feat"), P("feat", None), P("feat", None), P("dom", "feat")),
        check_vma=False,
    )
```

```python
import math

import jax
import jax.numpy as jnp
from jax import lax
from jax.experimental import pallas as pl
from jax.experimental.pallas import tpu as pltpu
from jax.sharding import PartitionSpec as P

F32 = jnp.float32
BF16 = jnp.bfloat16
MIB = 1 << 20


def dot(a, b, dims):
    return lax.dot_general(a, b, (dims, ((), ())), preferred_element_type=F32)


NN = ((1,), (0,))
NT = ((1,), (1,))
TN = ((0,), (0,))


def params(mib, steps):
    return pltpu.CompilerParams(
        dimension_semantics=("arbitrary",) * steps, vmem_limit_bytes=mib * MIB
    )


ANY = pl.BlockSpec(memory_space=pl.ANY)
HBM = pl.BlockSpec(memory_space=pltpu.HBM)
VMEM = pl.BlockSpec(memory_space=pltpu.VMEM)
SMEM = pl.BlockSpec(memory_space=pltpu.SMEM)


def own_copies(mib):
    return pltpu.CompilerParams(vmem_limit_bytes=mib * MIB)


def pack_kernel(send, hubs, feat, out, hub_rows, tails, sems):
    parts, height, width = out.shape
    edge = height - 8

    @pl.loop(0, parts // 8)
    def _(g):
        for i in range(8):
            q = g * 8 + i
            start = pl.multiple_of(send[q] * edge, edge)
            pltpu.make_async_copy(
                feat.at[pl.ds(start, edge), :], out.at[q, pl.ds(0, edge), :], sems.at[0]
            ).start()

    hub_rows[...] = jnp.zeros_like(hub_rows)
    for j in range(2):
        row = hubs[j]
        base = pl.multiple_of((row // 16) * 16, 16)
        block = feat[pl.ds(base, 16), :].astype(F32)
        here = lax.broadcasted_iota(jnp.int32, block.shape, 0) == row - base
        hub_rows[j : j + 1, :] = jnp.sum(jnp.where(here, block, 0.0), axis=0, keepdims=True)
    tails[...] = jnp.broadcast_to(hub_rows[...].astype(BF16)[None], tails.shape)
    tail = out.at[:, pl.ds(edge, 8), :]
    pltpu.make_async_copy(tails, tail, sems.at[1]).start()
    pltpu.make_async_copy(tails, tail, sems.at[1]).wait()
    body = out.at[:, pl.ds(0, edge), :]
    pltpu.make_async_copy(body, body, sems.at[0]).wait()


def pack(features, send_tile, hub_rows, edge):
    rows, width = features.shape
    parts = send_tile.shape[0]
    return pl.pallas_call(
        pack_kernel,
        name="pack",
        out_shape=jax.ShapeDtypeStruct((parts, edge + 8, width), BF16),
        grid_spec=pltpu.PrefetchScalarGridSpec(
            num_scalar_prefetch=2,
            grid=(1,),
            in_specs=[pl.BlockSpec((rows, width), lambda g, *_: (0, 0))],
            out_specs=HBM,
            scratch_shapes=[
                pltpu.VMEM((8, width), F32),
                pltpu.VMEM((parts, 8, width), BF16),
                pltpu.SemaphoreType.DMA((2,)),
            ],
        ),
        compiler_params=own_copies(58),
    )(send_tile, hub_rows, features)


def prepare_kernel(
    row, count, order, first, second, kinds, values, panel, *rest
):
    inv, flipped, pairs, squares = rest[-4:]
    step, steps = pl.program_id(0), pl.num_programs(0)
    edge = values.shape[1]
    slots, duos = flipped.shape[0], pairs.shape[0]

    @pl.when(step == 0)
    def _():
        squares[...] = jnp.zeros_like(squares)

    @pl.loop(0, slots)
    def _(i):
        k = step * slots + i
        flipped[i] = values[order[k]].T
        tile = values[k].astype(F32)
        live = (k < count[0]).astype(F32)
        start = pl.multiple_of(row[k] * edge, edge)
        squares[pl.ds(start, edge), :] += tile * tile * live

    @pl.loop(0, duos)
    def _(i):
        p = step * duos + i
        has_first = (kinds[p] > 0).astype(BF16)
        has_second = (kinds[p] > 1).astype(BF16)
        pairs[i, :, :edge] = values[first[p]] * has_first
        pairs[i, :, edge:] = values[second[p]] * has_second

    @pl.when(step == steps - 1)
    def _():
        @pl.loop(0, squares.shape[0] // edge)
        def _(t):
            at = pl.ds(pl.multiple_of(t * edge, edge), edge)
            wide = panel[at, :].astype(F32)
            wide = wide * wide
            half = wide.shape[1] // 2
            total = jnp.sum(
                squares[at, :] + wide[:, :half] + wide[:, half:], axis=1, keepdims=True
            )
            inv[at, :] = jnp.broadcast_to(lax.rsqrt(1.0 + total), (edge, inv.shape[1]))


def prepare(row, count, order, first, second, kinds, values, panel, duos, ready):
    slots, edge, _ = values.shape
    rows, hubs = panel.shape
    steps = 4
    whole = lambda g, *_: (0, 0)
    return pl.pallas_call(
        prepare_kernel,
        name="prepare",
        out_shape=(
            jax.ShapeDtypeStruct((rows, edge), F32),
            jax.ShapeDtypeStruct((slots, edge, edge), BF16),
            jax.ShapeDtypeStruct((duos, edge, 2 * edge), BF16),
        ),
        grid_spec=pltpu.PrefetchScalarGridSpec(
            num_scalar_prefetch=6,
            grid=(steps,),
            in_specs=[
                pl.BlockSpec((slots, edge, edge), lambda g, *_: (0, 0, 0)),
                pl.BlockSpec((rows, hubs), whole),
            ]
            + [ANY] * len(ready),
            out_specs=(
                pl.BlockSpec((rows, edge), whole),
                pl.BlockSpec((slots // steps, edge, edge), lambda g, *_: (g, 0, 0)),
                pl.BlockSpec((duos // steps, edge, 2 * edge), lambda g, *_: (g, 0, 0)),
            ),
            scratch_shapes=[pltpu.VMEM((rows, edge), F32)],
        ),
        compiler_params=params(40, 1),
        cost_estimate=pl.CostEstimate(
            flops=60_000_000_000, bytes_accessed=40_000_000, transcendentals=0
        ),
    )(row, count, order, first, second, kinds, values, panel, *ready)


DUO_STEP = 16


def gather_kernel(
    row, owner_a, owner_b, n_duos, pairs, incoming, panel, inv, out,
    tail, pan, tiles, norm, duos, tail_wide, hub_wide, sums, result, sems, duo_sems, out_sems,
):
    parts, edge, _ = tiles.shape
    rows = sums.shape[0]
    copy = pltpu.make_async_copy
    tail_in = copy(incoming.at[:, pl.ds(edge, 8), :], tail, sems.at[0])
    panel_in = copy(panel, pan, sems.at[1])
    tiles_in = copy(incoming.at[:, pl.ds(0, edge), :], tiles, sems.at[2])
    norm_in = copy(inv, norm, sems.at[3])
    steps = duos.shape[0] // DUO_STEP
    duo_in = [
        copy(pairs.at[pl.ds(c * DUO_STEP, DUO_STEP)], duos.at[pl.ds(c * DUO_STEP, DUO_STEP)], duo_sems.at[c])
        for c in range(steps)
    ]
    tail_in.start()
    panel_in.start()
    tiles_in.start()
    for c in range(steps):

        @pl.when(c * DUO_STEP < n_duos[0])
        def _():
            duo_in[c].start()

    norm_in.start()

    tail_in.wait()
    tail_wide[...] = tail[...].reshape(tail_wide.shape).astype(F32)
    for j in range(2):
        hub_wide[pl.ds(j, parts, stride=2), :] = tail_wide[pl.ds(j, parts, stride=8), :]
    hub_feats = hub_wide[...].astype(BF16)
    panel_in.wait()
    block = 512
    for t in range(rows // block):
        at = pl.ds(t * block, block)
        sums[at, :] = dot(pan[at, :], hub_feats, NN)
    tiles_in.wait()
    for c in range(steps):

        @pl.when(c * DUO_STEP < n_duos[0])
        def _():
            duo_in[c].wait()
            products = []
            for i in range(DUO_STEP):
                p = c * DUO_STEP + i
                columns = jnp.concatenate([tiles[owner_a[p]], tiles[owner_b[p]]], axis=0)
                products.append(dot(duos[p], columns, NN))
            for i in range(DUO_STEP):
                start = pl.multiple_of(row[c * DUO_STEP + i] * edge, edge)
                sums[pl.ds(start, edge), :] += products[i]

    norm_in.wait()
    block = rows // 4
    sent = []
    for t in range(4):
        at = pl.ds(t * block, block)
        result[at, :] = (sums[at, :] * norm[at, :]).astype(BF16)
        sent.append(copy(result.at[at, :], out.at[at, :], out_sems.at[t]))
        sent[-1].start()
    for s in sent:
        s.wait()


def gather(row, owner_a, owner_b, n_duos, pairs, incoming, panel, inv):
    duos, edge, _ = pairs.shape
    rows, hubs = panel.shape
    parts = incoming.shape[0]
    return pl.pallas_call(
        gather_kernel,
        name="gather",
        out_shape=jax.ShapeDtypeStruct((rows, edge), BF16),
        grid_spec=pltpu.PrefetchScalarGridSpec(
            num_scalar_prefetch=4,
            grid=(1,),
            in_specs=[ANY] * 4,
            out_specs=HBM,
            scratch_shapes=[
                pltpu.VMEM((parts, 8, edge), BF16),
                pltpu.VMEM((rows, hubs), BF16),
                pltpu.VMEM((parts, edge, edge), BF16),
                pltpu.VMEM((rows, edge), F32),
                pltpu.VMEM(pairs.shape, BF16),
                pltpu.VMEM((parts * 8, edge), F32),
                pltpu.VMEM((hubs, edge), F32),
                pltpu.VMEM((rows, edge), F32),
                pltpu.VMEM((rows, edge), BF16),
                pltpu.SemaphoreType.DMA((4,)),
                pltpu.SemaphoreType.DMA((duos // DUO_STEP,)),
                pltpu.SemaphoreType.DMA((4,)),
            ],
        ),
        compiler_params=own_copies(58),
    )(row, owner_a, owner_b, n_duos, pairs, incoming, panel, inv)


ROW_STEPS = 4
MID_MIB = 56
SLOT_STEP = 16


def middle_kernel(
    order_row, order_owner, count,
    feat, feat_peer, agg, agg_peer, cot, cot_peer, inv, panel, flipped, own_w, nbr_w,
    layer, slopes, terms,
    feat_v, feat_peer_v, agg_v, agg_peer_v, cot_v, cot_peer_v, inv_v, panel_v, flipped_v,
    layer_v, slopes_v, agg_slopes, terms_v, hub_acc, hub_wide, carry,
    in_sems, flip_sems, out_sems, term_sems,
):
    rows, half = feat_v.shape
    slots, edge, _ = flipped_v.shape
    parts = terms_v.shape[0]
    copy = pltpu.make_async_copy
    block = rows // ROW_STEPS
    sources = (feat, feat_peer, agg, agg_peer, cot, cot_peer, inv, panel)
    places = (feat_v, feat_peer_v, agg_v, agg_peer_v, cot_v, cot_peer_v, inv_v, panel_v)
    at = [pl.ds(t * block, block) for t in range(ROW_STEPS)]
    inputs = [
        [copy(s.at[at[t], :], d.at[at[t], :], in_sems.at[t, i]) for i, (s, d) in enumerate(zip(sources, places))]
        for t in range(ROW_STEPS)
    ]
    steps = slots // SLOT_STEP
    flips = [
        copy(flipped.at[pl.ds(b * SLOT_STEP, SLOT_STEP)], flipped_v.at[pl.ds(b * SLOT_STEP, SLOT_STEP)], flip_sems.at[b])
        for b in range(steps)
    ]
    for t in range(ROW_STEPS):
        for c in inputs[t]:
            c.start()
    for b in range(steps):

        @pl.when(b * SLOT_STEP < count[0])
        def _():
            flips[b].start()

    terms_v[:, :edge, :] = jnp.zeros((parts, edge, half), BF16)
    hub_wide[...] = jnp.zeros_like(hub_wide)
    carry[...] = jnp.zeros_like(carry)

    sent = []
    for t in range(ROW_STEPS):
        for c in inputs[t]:
            c.wait()
        here = at[t]
        preact = dot(
            jnp.concatenate([feat_v[here, :], feat_peer_v[here, :]], axis=1), own_w[...], NN
        ) + dot(jnp.concatenate([agg_v[here, :], agg_peer_v[here, :]], axis=1), nbr_w[...], NN)
        layer_v[here, :] = jnp.maximum(preact[:, :half], 0.0).astype(BF16)
        cotangent = jnp.concatenate([cot_v[here, :], cot_peer_v[here, :]], axis=1).astype(F32)
        slope = jnp.where(preact > 0, cotangent, 0.0).astype(BF16)
        slopes_v[here, :] = slope
        sent.append(copy(layer_v.at[here, :], layer.at[here, :], out_sems.at[t, 0]))
        sent.append(copy(slopes_v.at[here, :], slopes.at[here, :], out_sems.at[t, 1]))
        sent[-2].start()
        sent[-1].start()
        back = (dot(slope, nbr_w[:half, :], NT) * inv_v[here, :]).astype(BF16)
        agg_slopes[here, :] = back
        hub = dot(panel_v[here, :], back, TN)
        if t == 0:
            hub_acc[...] = hub
        else:
            hub_acc[...] += hub

    for j in range(2):
        hub_wide[pl.ds(j, parts, stride=8), :] = hub_acc[pl.ds(j, parts, stride=2), :]
    terms_v[:, edge:, :] = hub_wide[...].reshape(parts, 8, half).astype(BF16)

    group = parts // 8
    for b in range(steps):

        @pl.when(b * SLOT_STEP < count[0])
        def _():
            flips[b].wait()
            products = []
            for i in range(SLOT_STEP):
                k = b * SLOT_STEP + i
                start = pl.multiple_of(order_row[k] * edge, edge)
                products.append(dot(flipped_v[k], agg_slopes[pl.ds(start, edge), :], NN))
            total = carry[...]
            for i in range(SLOT_STEP):
                k = b * SLOT_STEP + i
                live = (k < count[0]).astype(F32)
                fresh = products[i] * live
                if k:
                    same = (order_owner[k] == order_owner[k - 1]).astype(F32)
                    total = fresh + total * same
                else:
                    total = fresh
                terms_v[order_owner[k], :edge, :] = total.astype(BF16)
            carry[...] = total
            first = order_owner[b * SLOT_STEP] // group if b else 0
            after = (b + 1) * SLOT_STEP
            last = jnp.where(
                after >= count[0], parts // group, order_owner[min(after, slots - 1)] // group
            )

            @pl.loop(first, last)
            def _(g):
                owners = pl.ds(g * group, group)
                copy(terms_v.at[owners], terms.at[owners], term_sems.at[0]).start()

    for c in sent:
        c.wait()
    copy(terms_v, terms, term_sems.at[0]).wait()


def middle(
    order_row, order_owner, count,
    feat, feat_peer, agg, agg_peer, cot, cot_peer, inv, panel, flipped, own_w, nbr_w, parts,
):
    rows, half = feat.shape
    hubs = panel.shape[1]
    edge = flipped.shape[1]
    narrow = pltpu.VMEM((rows, half), BF16)
    wide = pltpu.VMEM((rows, 2 * half), BF16)
    whole = lambda g, *_: (0, 0)
    height = edge + 8
    return pl.pallas_call(
        middle_kernel,
        name="middle",
        out_shape=(
            jax.ShapeDtypeStruct((rows, half), BF16),
            jax.ShapeDtypeStruct((rows, 2 * half), BF16),
            jax.ShapeDtypeStruct((parts, height, half), BF16),
        ),
        grid_spec=pltpu.PrefetchScalarGridSpec(
            num_scalar_prefetch=3,
            grid=(1,),
            in_specs=[ANY] * 9
            + [pl.BlockSpec(own_w.shape, whole), pl.BlockSpec(nbr_w.shape, whole)],
            out_specs=(HBM, HBM, HBM),
            scratch_shapes=[narrow] * 6
            + [
                pltpu.VMEM((rows, half), F32),
                pltpu.VMEM((rows, hubs), BF16),
                pltpu.VMEM(flipped.shape, BF16),
                narrow,
                wide,
                narrow,
                pltpu.VMEM((parts, height, half), BF16),
                pltpu.VMEM((hubs, half), F32),
                pltpu.VMEM((4 * hubs, half), F32),
                pltpu.VMEM((edge, half), F32),
                pltpu.SemaphoreType.DMA((ROW_STEPS, 8)),
                pltpu.SemaphoreType.DMA((flipped.shape[0] // SLOT_STEP,)),
                pltpu.SemaphoreType.DMA((ROW_STEPS, 2)),
                pltpu.SemaphoreType.DMA((1,)),
            ],
        ),
        compiler_params=own_copies(MID_MIB),
    )(
        order_row, order_owner, count,
        feat, feat_peer, agg, agg_peer, cot, cot_peer, inv, panel, flipped, own_w, nbr_w,
    )


def side_kernel(where, feat, agg, slopes, grads, acc):
    step, steps = pl.program_id(0), pl.num_programs(0)
    half = feat.shape[1]
    part = dot(jnp.concatenate([feat[...], agg[...]], axis=1), slopes[...], TN)

    @pl.when(step == 0)
    def _():
        acc[...] = part

    @pl.when(step > 0)
    def _():
        acc[...] += part

    @pl.when(step == steps - 1)
    def _():
        y, x = where[0] % 4, (where[0] // 4) % 4
        n = half // 4
        for c in range(4):
            for r in range(4):
                grads[jnp.bitwise_xor(c, y), jnp.bitwise_xor(r, x)] = acc[
                    (c // 2) * half + r * n : (c // 2) * half + (r + 1) * n,
                    (c % 2) * half : (c % 2 + 1) * half,
                ]


def side(where, feat, agg, slopes):
    rows, half = feat.shape
    block = 1024
    by_row = lambda width: pl.BlockSpec((block, width), lambda g, *_: (g, 0))
    return pl.pallas_call(
        side_kernel,
        name="side",
        out_shape=jax.ShapeDtypeStruct((4, 4, half // 4, half), F32),
        grid_spec=pltpu.PrefetchScalarGridSpec(
            num_scalar_prefetch=1,
            grid=(rows // block,),
            in_specs=[by_row(half), by_row(half), by_row(2 * half)],
            out_specs=pl.BlockSpec((4, 4, half // 4, half), lambda g, *_: (0, 0, 0, 0)),
            scratch_shapes=[pltpu.VMEM((2 * half, 2 * half), F32)],
        ),
        compiler_params=params(32, 1),
    )(where, feat, agg, slopes)


def direct_kernel(slopes, own_w, passed, direct, passed_out):
    passed_out[...] = passed[...]
    block = 512
    for t in range(slopes.shape[0] // block):
        at = pl.ds(t * block, block)
        direct[at, :] = dot(slopes[at, :], own_w[...], NT)


def direct_part(slopes, own_w, passed):
    return pl.pallas_call(
        direct_kernel,
        name="direct",
        out_shape=(
            jax.ShapeDtypeStruct((slopes.shape[0], own_w.shape[0]), F32),
            jax.ShapeDtypeStruct(passed.shape, passed.dtype),
        ),
        in_specs=[VMEM] * 3,
        out_specs=(VMEM, VMEM),
        compiler_params=own_copies(8),
    )(slopes, own_w, passed)


def finish_kernel(
    send, hubs, returned, direct, grads, out, grads_out, acc, landed, sems, part_sems
):
    parts, height, half = landed.shape
    edge = acc.shape[1]
    copy = pltpu.make_async_copy
    steps = 4
    group = parts // steps
    arrivals = [
        copy(returned.at[pl.ds(g * group, group)], landed.at[pl.ds(g * group, group)], part_sems.at[g])
        for g in range(steps)
    ]
    for c in arrivals:
        c.start()
    grads_out[...] = grads[...]
    acc[...] = direct[...]
    share = jnp.zeros((8, half), F32)
    for g in range(steps):
        arrivals[g].wait()
        for i in range(group):
            p = g * group + i
            acc[send[p]] += landed[p, :edge, :].astype(F32)
            share = share + landed[p, edge:, :].astype(F32)
    for j in range(2):
        row = hubs[j]
        tile, inside = row // edge, row % edge
        base = pl.multiple_of((inside // 8) * 8, 8)
        here = lax.broadcasted_iota(jnp.int32, (8, half), 0) == inside - base
        acc[tile, pl.ds(base, 8), :] += jnp.where(here, share[j : j + 1, :], 0.0)
    end = copy(acc, out, sems.at[0])
    end.start()
    end.wait()


def finish(send_tile, hub_rows, returned, direct, grads):
    return pl.pallas_call(
        finish_kernel,
        name="finish",
        out_shape=(
            jax.ShapeDtypeStruct(direct.shape, F32),
            jax.ShapeDtypeStruct(grads.shape, F32),
        ),
        in_specs=[SMEM, SMEM, ANY, VMEM, VMEM],
        out_specs=(HBM, VMEM),
        scratch_shapes=[
            pltpu.VMEM(direct.shape, F32),
            pltpu.VMEM(returned.shape, BF16),
            pltpu.SemaphoreType.DMA((1,)),
            pltpu.SemaphoreType.DMA((4,)),
        ],
        compiler_params=own_copies(16),
    )(send_tile, hub_rows, returned, direct, grads)


def place_kernel(factor, where, own, one, two, three, self_grad, neighbor_grad, blocks):
    for m, group in enumerate((own, one, two, three)):
        blocks[m] = group[...]
    y, x, core = where[0] % 4, (where[0] // 4) % 4, where[1]
    n, half = blocks.shape[2:]
    for j, out in enumerate((self_grad, neighbor_grad)):
        for c in range(2):
            column = 2 * j + jnp.bitwise_xor(c, core)
            for r in range(4):
                out[r * n : (r + 1) * n, c * half : (c + 1) * half] = (
                    blocks[jnp.bitwise_xor(column, y), jnp.bitwise_xor(r, x)] * factor
                )


def put_in_place(where, groups, factor):
    four, n, half = groups[0].shape
    out = jax.ShapeDtypeStruct((four * n, 2 * half), F32)
    return pl.pallas_call(
        lambda *refs: place_kernel(factor, *refs),
        name="place",
        out_shape=(out, out),
        in_specs=[SMEM] + [VMEM] * 4,
        out_specs=(VMEM, VMEM),
        scratch_shapes=[pltpu.VMEM((4, four, n, half), F32)],
        compiler_params=own_copies(8),
    )(where, *groups)


def plan(tile_row, tile_owner, tile_count, tiles, parts):
    slots = tile_row.shape[0]
    index = jnp.arange(slots, dtype=jnp.int32)
    live = index < tile_count[0]
    earlier = index[None, :] < index[:, None]
    pick = lambda where, what: jnp.sum(jnp.where(where, what, 0), axis=1, dtype=jnp.int32)

    key = jnp.where(live, tile_owner, parts)
    before = (key[None, :] < key[:, None]) | ((key[None, :] == key[:, None]) & earlier)
    rank = jnp.sum(before, axis=1, dtype=jnp.int32)
    last = jnp.minimum(index, tile_count[0] - 1)
    at = rank[None, :] == last[:, None]
    order = pick(at, index[None, :])
    order_row = pick(at, tile_row[None, :])
    order_owner = pick(at, tile_owner[None, :])

    mates = live[None, :] & (tile_row[None, :] == tile_row[:, None])
    inside = jnp.sum(mates & earlier, axis=1, dtype=jnp.int32)
    rows = jnp.arange(tiles, dtype=jnp.int32)
    per_row = jnp.sum(live[None, :] & (tile_row[None, :] == rows[:, None]), axis=1, dtype=jnp.int32)
    row_pairs = (per_row + 1) // 2
    lower = jnp.sum(
        jnp.where(rows[None, :] < tile_row[:, None], row_pairs[None, :], 0), axis=1, dtype=jnp.int32
    )
    pair = jnp.where(live, lower + inside // 2, -1)
    duos = (slots + tiles) // 2
    p = jnp.arange(duos, dtype=jnp.int32)
    is_first = (pair[None, :] == p[:, None]) & (inside[None, :] % 2 == 0)
    is_second = (pair[None, :] == p[:, None]) & (inside[None, :] % 2 == 1)
    first = pick(is_first, index[None, :])
    second = pick(is_second, index[None, :])
    owner_a = pick(is_first, tile_owner[None, :])
    owner_b = pick(is_second, tile_owner[None, :])
    pair_row = pick(is_first, tile_row[None, :])
    kinds = pick(is_first, 1) + pick(is_second, 1)
    n_duos = jnp.sum(row_pairs, dtype=jnp.int32).reshape(1)
    return (
        (order, order_row, order_owner),
        (first, second, kinds, pair_row, owner_a, owner_b, n_duos),
        duos,
    )


def exchange(block):
    return lax.all_to_all(block, "dom", split_axis=0, concat_axis=0, tiled=True)


def swap(block):
    return lax.ppermute(block, "feat", [(0, 1), (1, 0)])


def move(block, axis, bits):
    shift = {"z": 4, "x": 2, "y": 0}[axis]
    pairs = [(d, d ^ (bits << shift)) for d in range(lax.axis_size("dom"))]
    return lax.ppermute(block, "dom", pairs)


def moved_three(blocks, axis):
    return [move(blocks[i], axis, i) for i in (1, 2, 3)]


def total(own, near):
    return (own + near[0]) + (near[1] + near[2])


def shards(
    features,
    self_weight,
    neighbor_weight,
    tile_values,
    tile_row,
    tile_owner,
    send_tile,
    tile_count,
    hub_panel,
    hub_rows,
    cotangent,
):
    rows_dev, half = features.shape
    tile_edge = tile_values.shape[1]
    tiles_dev = rows_dev // tile_edge
    dom_size = lax.axis_size("dom")
    core = lax.axis_index("feat")

    outgoing = pack(features, send_tile, hub_rows, tile_edge)
    incoming = exchange(outgoing)

    def own_first(w):
        return jnp.where(core == 0, w, jnp.concatenate([w[:, half:], w[:, :half]], axis=1))

    weights = own_first(jnp.concatenate([self_weight, neighbor_weight], axis=0))
    peer_weights = swap(weights)
    peer_weights = jnp.concatenate([peer_weights[:, half:], peer_weights[:, :half]], axis=1)
    own_w = jnp.concatenate([weights[:half], peer_weights[:half]], axis=0)
    nbr_w = jnp.concatenate([weights[half:], peer_weights[half:]], axis=0)
    feat_peer = swap(features)
    cot_peer = swap(cotangent)

    by_owner, by_row, duos = plan(tile_row, tile_owner, tile_count, tiles_dev, dom_size)
    order, order_row, order_owner = by_owner
    first, second, kinds, pair_row, owner_a, owner_b, n_duos = by_row
    inv, flipped, pairs = prepare(
        tile_row, tile_count, order, first, second, kinds, tile_values, hub_panel, duos,
        (own_w, nbr_w, feat_peer, cot_peer),
    )

    aggregate = gather(pair_row, owner_a, owner_b, n_duos, pairs, incoming, hub_panel, inv)
    agg_peer = swap(aggregate)
    layer_out, slopes, terms = middle(
        order_row, order_owner, tile_count,
        features, feat_peer, aggregate, agg_peer, cotangent, cot_peer, inv, hub_panel, flipped,
        own_w, nbr_w, dom_size,
    )
    returned = exchange(terms)

    where = jnp.stack([lax.axis_index("dom").astype(jnp.int32), core.astype(jnp.int32)])
    grads = side(where, features, aggregate, slopes)
    grads = total(grads[0], moved_three(grads, "y"))
    direct, grads = direct_part(slopes, own_w[:half], grads)
    grads = total(grads[0], moved_three(grads, "x"))
    grads = total(grads, [move(grads, "z", i) for i in (1, 2, 3)])
    grads = grads + move(grads, "z", 4)
    grads = jnp.stack([grads] + [move(grads, "x", i) for i in (1, 2, 3)])
    near = [move(grads, "y", i) for i in (1, 2, 3)]
    input_grad, grads = finish(
        send_tile, hub_rows, returned, direct.reshape(tiles_dev, tile_edge, half), grads
    )
    input_grad = input_grad.reshape(rows_dev, half)
    self_grad, neighbor_grad = put_in_place(
        where, [grads] + near, 1.0 / math.sqrt(rows_dev * dom_size)
    )
    return (layer_out, self_grad, neighbor_grad, input_grad)


def solution(mesh):
    placed = (
        P("dom", "feat"),
        P("feat", None),
        P("feat", None),
        P("dom", None, None),
        P("dom"),
        P("dom"),
        P("dom"),
        P("dom"),
        P("dom", None),
        P("dom"),
        P("dom", "feat"),
    )
    return jax.shard_map(
        shards,
        mesh=mesh,
        in_specs=placed,
        out_specs=(P("dom", "feat"), P("feat", None), P("feat", None), P("dom", "feat")),
        check_vma=False,
    )
```

```python
import math

import jax
import jax.numpy as jnp
from jax import lax
from jax.experimental import pallas as pl
from jax.experimental.pallas import tpu as pltpu
from jax.sharding import PartitionSpec as P

F32 = jnp.float32
BF16 = jnp.bfloat16
MIB = 1 << 20


def dot(a, b, dims):
    return lax.dot_general(a, b, (dims, ((), ())), preferred_element_type=F32)


NN = ((1,), (0,))
NT = ((1,), (1,))
TN = ((0,), (0,))


def params(mib, steps):
    return pltpu.CompilerParams(
        dimension_semantics=("arbitrary",) * steps, vmem_limit_bytes=mib * MIB
    )


ANY = pl.BlockSpec(memory_space=pl.ANY)
HBM = pl.BlockSpec(memory_space=pltpu.HBM)
VMEM = pl.BlockSpec(memory_space=pltpu.VMEM)
SMEM = pl.BlockSpec(memory_space=pltpu.SMEM)


def own_copies(mib):
    return pltpu.CompilerParams(vmem_limit_bytes=mib * MIB)


def pack_kernel(send, hubs, feat, out, hub_rows, tails, sems):
    parts, height, width = out.shape
    edge = height - 8

    @pl.loop(0, parts // 8)
    def _(g):
        for i in range(8):
            q = g * 8 + i
            start = pl.multiple_of(send[q] * edge, edge)
            pltpu.make_async_copy(
                feat.at[pl.ds(start, edge), :], out.at[q, pl.ds(0, edge), :], sems.at[0]
            ).start()

    hub_rows[...] = jnp.zeros_like(hub_rows)
    for j in range(2):
        row = hubs[j]
        base = pl.multiple_of((row // 16) * 16, 16)
        block = feat[pl.ds(base, 16), :].astype(F32)
        here = lax.broadcasted_iota(jnp.int32, block.shape, 0) == row - base
        hub_rows[j : j + 1, :] = jnp.sum(jnp.where(here, block, 0.0), axis=0, keepdims=True)
    tails[...] = jnp.broadcast_to(hub_rows[...].astype(BF16)[None], tails.shape)
    tail = out.at[:, pl.ds(edge, 8), :]
    pltpu.make_async_copy(tails, tail, sems.at[1]).start()
    pltpu.make_async_copy(tails, tail, sems.at[1]).wait()
    body = out.at[:, pl.ds(0, edge), :]
    pltpu.make_async_copy(body, body, sems.at[0]).wait()


def pack(features, send_tile, hub_rows, edge):
    rows, width = features.shape
    parts = send_tile.shape[0]
    return pl.pallas_call(
        pack_kernel,
        name="pack",
        out_shape=jax.ShapeDtypeStruct((parts, edge + 8, width), BF16),
        grid_spec=pltpu.PrefetchScalarGridSpec(
            num_scalar_prefetch=2,
            grid=(1,),
            in_specs=[pl.BlockSpec((rows, width), lambda g, *_: (0, 0))],
            out_specs=HBM,
            scratch_shapes=[
                pltpu.VMEM((8, width), F32),
                pltpu.VMEM((parts, 8, width), BF16),
                pltpu.SemaphoreType.DMA((2,)),
            ],
        ),
        compiler_params=own_copies(58),
    )(send_tile, hub_rows, features)


def prepare_kernel(
    row, count, order, first, second, kinds, values, panel, *rest
):
    inv, flipped, pairs, panel_t, squares = rest[-5:]
    step, steps = pl.program_id(0), pl.num_programs(0)
    edge = values.shape[1]
    slots, duos = flipped.shape[0], pairs.shape[0]

    @pl.when(step == 0)
    def _():
        squares[...] = jnp.zeros_like(squares)

    @pl.loop(0, slots)
    def _(i):
        k = step * slots + i
        flipped[i] = values[order[k]].T
        tile = values[k].astype(F32)
        live = (k < count[0]).astype(F32)
        start = pl.multiple_of(row[k] * edge, edge)
        squares[pl.ds(start, edge), :] += tile * tile * live

    @pl.loop(0, duos)
    def _(i):
        p = step * duos + i
        has_first = (kinds[p] > 0).astype(BF16)
        has_second = (kinds[p] > 1).astype(BF16)
        pairs[i, :, :edge] = values[first[p]] * has_first
        pairs[i, :, edge:] = values[second[p]] * has_second

    @pl.when(step == steps - 1)
    def _():
        @pl.loop(0, squares.shape[0] // edge)
        def _(t):
            at = pl.ds(pl.multiple_of(t * edge, edge), edge)
            panel_t[:, at] = panel[at, :].T
            wide = panel[at, :].astype(F32)
            wide = wide * wide
            half = wide.shape[1] // 2
            total = jnp.sum(
                squares[at, :] + wide[:, :half] + wide[:, half:], axis=1, keepdims=True
            )
            inv[at, :] = jnp.broadcast_to(lax.rsqrt(1.0 + total), (edge, inv.shape[1]))


def prepare(row, count, order, first, second, kinds, values, panel, duos, ready):
    slots, edge, _ = values.shape
    rows, hubs = panel.shape
    steps = 4
    whole = lambda g, *_: (0, 0)
    return pl.pallas_call(
        prepare_kernel,
        name="prepare",
        out_shape=(
            jax.ShapeDtypeStruct((rows, edge), F32),
            jax.ShapeDtypeStruct((slots, edge, edge), BF16),
            jax.ShapeDtypeStruct((duos, edge, 2 * edge), BF16),
            jax.ShapeDtypeStruct((hubs, rows), BF16),
        ),
        grid_spec=pltpu.PrefetchScalarGridSpec(
            num_scalar_prefetch=6,
            grid=(steps,),
            in_specs=[
                pl.BlockSpec((slots, edge, edge), lambda g, *_: (0, 0, 0)),
                pl.BlockSpec((rows, hubs), whole),
            ]
            + [ANY] * len(ready),
            out_specs=(
                pl.BlockSpec((rows, edge), whole),
                pl.BlockSpec((slots // steps, edge, edge), lambda g, *_: (g, 0, 0)),
                pl.BlockSpec((duos // steps, edge, 2 * edge), lambda g, *_: (g, 0, 0)),
                pl.BlockSpec((hubs, rows), whole),
            ),
            scratch_shapes=[pltpu.VMEM((rows, edge), F32)],
        ),
        compiler_params=params(40, 1),
        cost_estimate=pl.CostEstimate(
            flops=60_000_000_000, bytes_accessed=40_000_000, transcendentals=0
        ),
    )(row, count, order, first, second, kinds, values, panel, *ready)


DUO_STEP = 16


def gather_kernel(
    row, owner_a, owner_b, n_duos, pairs, incoming, panel, inv, out,
    tail, pan, tiles, norm, duos, tail_wide, hub_wide, sums, result, sems, duo_sems, out_sems,
):
    parts, edge, _ = tiles.shape
    rows = sums.shape[0]
    copy = pltpu.make_async_copy
    tail_in = copy(incoming.at[:, pl.ds(edge, 8), :], tail, sems.at[0])
    panel_in = copy(panel, pan, sems.at[1])
    tiles_in = copy(incoming.at[:, pl.ds(0, edge), :], tiles, sems.at[2])
    norm_in = copy(inv, norm, sems.at[3])
    steps = duos.shape[0] // DUO_STEP
    duo_in = [
        copy(pairs.at[pl.ds(c * DUO_STEP, DUO_STEP)], duos.at[pl.ds(c * DUO_STEP, DUO_STEP)], duo_sems.at[c])
        for c in range(steps)
    ]
    tail_in.start()
    panel_in.start()
    tiles_in.start()
    for c in range(steps):

        @pl.when(c * DUO_STEP < n_duos[0])
        def _():
            duo_in[c].start()

    norm_in.start()

    tail_in.wait()
    tail_wide[...] = tail[...].reshape(tail_wide.shape).astype(F32)
    for j in range(2):
        hub_wide[pl.ds(j, parts, stride=2), :] = tail_wide[pl.ds(j, parts, stride=8), :]
    hub_feats = hub_wide[...].astype(BF16)
    panel_in.wait()
    block = 512
    for t in range(rows // block):
        at = pl.ds(t * block, block)
        sums[at, :] = dot(pan[at, :], hub_feats, NN)
    tiles_in.wait()
    for c in range(steps):

        @pl.when(c * DUO_STEP < n_duos[0])
        def _():
            duo_in[c].wait()
            products = []
            for i in range(DUO_STEP):
                p = c * DUO_STEP + i
                columns = jnp.concatenate([tiles[owner_a[p]], tiles[owner_b[p]]], axis=0)
                products.append(dot(duos[p], columns, NN))
            for i in range(DUO_STEP):
                start = pl.multiple_of(row[c * DUO_STEP + i] * edge, edge)
                sums[pl.ds(start, edge), :] += products[i]

    norm_in.wait()
    block = rows // 4
    sent = []
    for t in range(4):
        at = pl.ds(t * block, block)
        result[at, :] = (sums[at, :] * norm[at, :]).astype(BF16)
        sent.append(copy(result.at[at, :], out.at[at, :], out_sems.at[t]))
        sent[-1].start()
    for s in sent:
        s.wait()


def gather(row, owner_a, owner_b, n_duos, pairs, incoming, panel, inv):
    duos, edge, _ = pairs.shape
    rows, hubs = panel.shape
    parts = incoming.shape[0]
    return pl.pallas_call(
        gather_kernel,
        name="gather",
        out_shape=jax.ShapeDtypeStruct((rows, edge), BF16),
        grid_spec=pltpu.PrefetchScalarGridSpec(
            num_scalar_prefetch=4,
            grid=(1,),
            in_specs=[ANY] * 4,
            out_specs=HBM,
            scratch_shapes=[
                pltpu.VMEM((parts, 8, edge), BF16),
                pltpu.VMEM((rows, hubs), BF16),
                pltpu.VMEM((parts, edge, edge), BF16),
                pltpu.VMEM((rows, edge), F32),
                pltpu.VMEM(pairs.shape, BF16),
                pltpu.VMEM((parts * 8, edge), F32),
                pltpu.VMEM((hubs, edge), F32),
                pltpu.VMEM((rows, edge), F32),
                pltpu.VMEM((rows, edge), BF16),
                pltpu.SemaphoreType.DMA((4,)),
                pltpu.SemaphoreType.DMA((duos // DUO_STEP,)),
                pltpu.SemaphoreType.DMA((4,)),
            ],
        ),
        compiler_params=own_copies(58),
    )(row, owner_a, owner_b, n_duos, pairs, incoming, panel, inv)


ROW_STEPS = 4
MID_MIB = 56
SLOT_STEP = 16


def middle_kernel(
    order_row, order_owner, count,
    feat, feat_peer, agg, agg_peer, cot, cot_peer, inv, panel_t, flipped, own_w, nbr_w,
    terms,
    feat_v, feat_peer_v, agg_v, agg_peer_v, cot_v, cot_peer_v, inv_v, panel_v, flipped_v,
    agg_slopes, terms_v, hub_acc, hub_wide, carry, in_sems, flip_sems, term_sems,
):
    rows, half = feat_v.shape
    slots, edge, _ = flipped_v.shape
    parts = terms_v.shape[0]
    copy = pltpu.make_async_copy
    block = rows // ROW_STEPS
    sources = (feat, feat_peer, agg, agg_peer, cot, cot_peer, inv)
    places = (feat_v, feat_peer_v, agg_v, agg_peer_v, cot_v, cot_peer_v, inv_v)
    at = [pl.ds(t * block, block) for t in range(ROW_STEPS)]
    inputs = [
        [copy(s.at[at[t], :], d.at[at[t], :], in_sems.at[t, i]) for i, (s, d) in enumerate(zip(sources, places))]
        + [copy(panel_t.at[:, at[t]], panel_v.at[:, at[t]], in_sems.at[t, 7])]
        for t in range(ROW_STEPS)
    ]
    steps = slots // SLOT_STEP
    flips = [
        copy(flipped.at[pl.ds(b * SLOT_STEP, SLOT_STEP)], flipped_v.at[pl.ds(b * SLOT_STEP, SLOT_STEP)], flip_sems.at[b])
        for b in range(steps)
    ]
    for t in range(ROW_STEPS):
        for c in inputs[t]:
            c.start()
    for b in range(steps):

        @pl.when(b * SLOT_STEP < count[0])
        def _():
            flips[b].start()

    terms_v[:, :edge, :] = jnp.zeros((parts, edge, half), BF16)
    hub_wide[...] = jnp.zeros_like(hub_wide)
    carry[...] = jnp.zeros_like(carry)

    for t in range(ROW_STEPS):
        for c in inputs[t]:
            c.wait()
        here = at[t]
        preact = dot(
            jnp.concatenate([feat_v[here, :], feat_peer_v[here, :]], axis=1), own_w[...], NN
        ) + dot(jnp.concatenate([agg_v[here, :], agg_peer_v[here, :]], axis=1), nbr_w[...], NN)
        cotangent = jnp.concatenate([cot_v[here, :], cot_peer_v[here, :]], axis=1).astype(F32)
        slope = jnp.where(preact > 0, cotangent, 0.0).astype(BF16)
        back = (dot(slope, nbr_w[:half, :], NT) * inv_v[here, :]).astype(BF16)
        agg_slopes[here, :] = back
        hub = dot(panel_v[:, here], back, NN)
        if t == 0:
            hub_acc[...] = hub
        else:
            hub_acc[...] += hub

    for j in range(2):
        hub_wide[pl.ds(j, parts, stride=8), :] = hub_acc[pl.ds(j, parts, stride=2), :]
    terms_v[:, edge:, :] = hub_wide[...].reshape(parts, 8, half).astype(BF16)

    group = parts // 8
    for b in range(steps):

        @pl.when(b * SLOT_STEP < count[0])
        def _():
            flips[b].wait()
            products = []
            for i in range(SLOT_STEP):
                k = b * SLOT_STEP + i
                start = pl.multiple_of(order_row[k] * edge, edge)
                products.append(dot(flipped_v[k], agg_slopes[pl.ds(start, edge), :], NN))
            total = carry[...]
            for i in range(SLOT_STEP):
                k = b * SLOT_STEP + i
                live = (k < count[0]).astype(F32)
                fresh = products[i] * live
                if k:
                    same = (order_owner[k] == order_owner[k - 1]).astype(F32)
                    total = fresh + total * same
                else:
                    total = fresh
                terms_v[order_owner[k], :edge, :] = total.astype(BF16)
            carry[...] = total
            first = order_owner[b * SLOT_STEP] // group if b else 0
            after = (b + 1) * SLOT_STEP
            last = jnp.where(
                after >= count[0], parts // group, order_owner[min(after, slots - 1)] // group
            )

            @pl.loop(first, last)
            def _(g):
                owners = pl.ds(g * group, group)
                copy(terms_v.at[owners], terms.at[owners], term_sems.at[0]).start()

    copy(terms_v, terms, term_sems.at[0]).wait()


def middle(
    order_row, order_owner, count,
    feat, feat_peer, agg, agg_peer, cot, cot_peer, inv, panel_t, flipped, own_w, nbr_w, parts,
):
    rows, half = feat.shape
    hubs = panel_t.shape[0]
    edge = flipped.shape[1]
    narrow = pltpu.VMEM((rows, half), BF16)
    whole = lambda g, *_: (0, 0)
    height = edge + 8
    return pl.pallas_call(
        middle_kernel,
        name="middle",
        out_shape=jax.ShapeDtypeStruct((parts, height, half), BF16),
        grid_spec=pltpu.PrefetchScalarGridSpec(
            num_scalar_prefetch=3,
            grid=(1,),
            in_specs=[ANY] * 9
            + [pl.BlockSpec(own_w.shape, whole), pl.BlockSpec(nbr_w.shape, whole)],
            out_specs=HBM,
            scratch_shapes=[narrow] * 6
            + [
                pltpu.VMEM((rows, half), F32),
                pltpu.VMEM((hubs, rows), BF16),
                pltpu.VMEM(flipped.shape, BF16),
                narrow,
                pltpu.VMEM((parts, height, half), BF16),
                pltpu.VMEM((hubs, half), F32),
                pltpu.VMEM((4 * hubs, half), F32),
                pltpu.VMEM((edge, half), F32),
                pltpu.SemaphoreType.DMA((ROW_STEPS, 8)),
                pltpu.SemaphoreType.DMA((flipped.shape[0] // SLOT_STEP,)),
                pltpu.SemaphoreType.DMA((1,)),
            ],
        ),
        compiler_params=own_copies(MID_MIB),
    )(
        order_row, order_owner, count,
        feat, feat_peer, agg, agg_peer, cot, cot_peer, inv, panel_t, flipped, own_w, nbr_w,
    )


def side_kernel(
    where, feat, feat_peer, agg, agg_peer, cot, cot_peer, own_w, nbr_w, layer, slopes, grads, acc
):
    step, steps = pl.program_id(0), pl.num_programs(0)
    half = feat.shape[1]
    x, a = feat[...], agg[...]
    preact = dot(jnp.concatenate([x, feat_peer[...]], axis=1), own_w[...], NN) + dot(
        jnp.concatenate([a, agg_peer[...]], axis=1), nbr_w[...], NN
    )
    layer[...] = jnp.maximum(preact[:, :half], 0.0).astype(BF16)
    cotangent = jnp.concatenate([cot[...], cot_peer[...]], axis=1).astype(F32)
    slope = jnp.where(preact > 0, cotangent, 0.0).astype(BF16)
    slopes[...] = slope
    part = dot(jnp.concatenate([x, a], axis=1), slope, TN)

    @pl.when(step == 0)
    def _():
        acc[...] = part

    @pl.when(step > 0)
    def _():
        acc[...] += part

    @pl.when(step == steps - 1)
    def _():
        y = where[0] % 4
        for c in range(4):
            grads[jnp.bitwise_xor(c, y)] = acc[
                (c // 2) * half : (c // 2 + 1) * half, (c % 2) * half : (c % 2 + 1) * half
            ]


def side(where, feat, feat_peer, agg, agg_peer, cot, cot_peer, own_w, nbr_w, after):
    rows, half = feat.shape
    block = rows // ROW_STEPS
    by_row = lambda width: pl.BlockSpec((block, width), lambda g, *_: (g, 0))
    whole = lambda g, *_: (0, 0)
    return pl.pallas_call(
        lambda *refs: side_kernel(*refs[:9], *refs[10:]),
        name="side",
        out_shape=(
            jax.ShapeDtypeStruct((rows, half), BF16),
            jax.ShapeDtypeStruct((rows, 2 * half), BF16),
            jax.ShapeDtypeStruct((4, half, half), F32),
        ),
        grid_spec=pltpu.PrefetchScalarGridSpec(
            num_scalar_prefetch=1,
            grid=(rows // block,),
            in_specs=[by_row(half)] * 6
            + [pl.BlockSpec(own_w.shape, whole), pl.BlockSpec(nbr_w.shape, whole), ANY],
            out_specs=(
                by_row(half),
                by_row(2 * half),
                pl.BlockSpec((4, half, half), lambda g, *_: (0, 0, 0)),
            ),
            scratch_shapes=[pltpu.VMEM((2 * half, 2 * half), F32)],
        ),
        compiler_params=params(32, 1),
    )(where, feat, feat_peer, agg, agg_peer, cot, cot_peer, own_w, nbr_w, after)


def direct_kernel(slopes, own_w, passed, direct, passed_out):
    passed_out[...] = passed[...]
    block = 512
    for t in range(slopes.shape[0] // block):
        at = pl.ds(t * block, block)
        direct[at, :] = dot(slopes[at, :], own_w[...], NT)


def direct_part(slopes, own_w, passed):
    return pl.pallas_call(
        direct_kernel,
        name="direct",
        out_shape=(
            jax.ShapeDtypeStruct((slopes.shape[0], own_w.shape[0]), F32),
            jax.ShapeDtypeStruct(passed.shape, passed.dtype),
        ),
        in_specs=[VMEM] * 3,
        out_specs=(VMEM, VMEM),
        compiler_params=own_copies(8),
    )(slopes, own_w, passed)


def finish_kernel(
    send, hubs, returned, direct, grads, out, grads_out, acc, landed, sems, part_sems
):
    parts, height, half = landed.shape
    edge = acc.shape[1]
    copy = pltpu.make_async_copy
    steps = 4
    group = parts // steps
    arrivals = [
        copy(returned.at[pl.ds(g * group, group)], landed.at[pl.ds(g * group, group)], part_sems.at[g])
        for g in range(steps)
    ]
    for c in arrivals:
        c.start()
    grads_out[...] = grads[...]
    acc[...] = direct[...]
    share = jnp.zeros((8, half), F32)
    for g in range(steps):
        arrivals[g].wait()
        for i in range(group):
            p = g * group + i
            acc[send[p]] += landed[p, :edge, :].astype(F32)
            share = share + landed[p, edge:, :].astype(F32)
    for j in range(2):
        row = hubs[j]
        tile, inside = row // edge, row % edge
        base = pl.multiple_of((inside // 8) * 8, 8)
        here = lax.broadcasted_iota(jnp.int32, (8, half), 0) == inside - base
        acc[tile, pl.ds(base, 8), :] += jnp.where(here, share[j : j + 1, :], 0.0)
    end = copy(acc, out, sems.at[0])
    end.start()
    end.wait()


def finish(send_tile, hub_rows, returned, direct, grads):
    return pl.pallas_call(
        finish_kernel,
        name="finish",
        out_shape=(
            jax.ShapeDtypeStruct(direct.shape, F32),
            jax.ShapeDtypeStruct(grads.shape, F32),
        ),
        in_specs=[SMEM, SMEM, ANY, VMEM, VMEM],
        out_specs=(HBM, VMEM),
        scratch_shapes=[
            pltpu.VMEM(direct.shape, F32),
            pltpu.VMEM(returned.shape, BF16),
            pltpu.SemaphoreType.DMA((1,)),
            pltpu.SemaphoreType.DMA((4,)),
        ],
        compiler_params=own_copies(16),
    )(send_tile, hub_rows, returned, direct, grads)


def place_kernel(factor, where, own, one, two, three, self_grad, neighbor_grad, blocks):
    for m, group in enumerate((own, one, two, three)):
        blocks[m] = group[...]
    y, core = where[0] % 4, where[1]
    half = blocks.shape[2]
    for j, out in enumerate((self_grad, neighbor_grad)):
        for c in range(2):
            column = 2 * j + jnp.bitwise_xor(c, core)
            out[:, c * half : (c + 1) * half] = blocks[jnp.bitwise_xor(column, y)] * factor


def put_in_place(where, groups, factor):
    rows, half = groups[0].shape
    out = jax.ShapeDtypeStruct((rows, 2 * half), F32)
    return pl.pallas_call(
        lambda *refs: place_kernel(factor, *refs),
        name="place",
        out_shape=(out, out),
        in_specs=[SMEM] + [VMEM] * 4,
        out_specs=(VMEM, VMEM),
        scratch_shapes=[pltpu.VMEM((4, rows, half), F32)],
        compiler_params=own_copies(8),
    )(where, *groups)


def plan(tile_row, tile_owner, tile_count, tiles, parts):
    slots = tile_row.shape[0]
    index = jnp.arange(slots, dtype=jnp.int32)
    live = index < tile_count[0]
    earlier = index[None, :] < index[:, None]
    pick = lambda where, what: jnp.sum(jnp.where(where, what, 0), axis=1, dtype=jnp.int32)

    key = jnp.where(live, tile_owner, parts)
    before = (key[None, :] < key[:, None]) | ((key[None, :] == key[:, None]) & earlier)
    rank = jnp.sum(before, axis=1, dtype=jnp.int32)
    last = jnp.minimum(index, tile_count[0] - 1)
    at = rank[None, :] == last[:, None]
    order = pick(at, index[None, :])
    order_row = pick(at, tile_row[None, :])
    order_owner = pick(at, tile_owner[None, :])

    mates = live[None, :] & (tile_row[None, :] == tile_row[:, None])
    inside = jnp.sum(mates & earlier, axis=1, dtype=jnp.int32)
    rows = jnp.arange(tiles, dtype=jnp.int32)
    per_row = jnp.sum(live[None, :] & (tile_row[None, :] == rows[:, None]), axis=1, dtype=jnp.int32)
    row_pairs = (per_row + 1) // 2
    lower = jnp.sum(
        jnp.where(rows[None, :] < tile_row[:, None], row_pairs[None, :], 0), axis=1, dtype=jnp.int32
    )
    pair = jnp.where(live, lower + inside // 2, -1)
    duos = (slots + tiles) // 2
    p = jnp.arange(duos, dtype=jnp.int32)
    is_first = (pair[None, :] == p[:, None]) & (inside[None, :] % 2 == 0)
    is_second = (pair[None, :] == p[:, None]) & (inside[None, :] % 2 == 1)
    first = pick(is_first, index[None, :])
    second = pick(is_second, index[None, :])
    owner_a = pick(is_first, tile_owner[None, :])
    owner_b = pick(is_second, tile_owner[None, :])
    pair_row = pick(is_first, tile_row[None, :])
    kinds = pick(is_first, 1) + pick(is_second, 1)
    n_duos = jnp.sum(row_pairs, dtype=jnp.int32).reshape(1)
    return (
        (order, order_row, order_owner),
        (first, second, kinds, pair_row, owner_a, owner_b, n_duos),
        duos,
    )


def exchange(block):
    return lax.all_to_all(block, "dom", split_axis=0, concat_axis=0, tiled=True)


def swap(block):
    return lax.ppermute(block, "feat", [(0, 1), (1, 0)])


def move(block, axis, bits):
    shift = {"z": 4, "x": 2, "y": 0}[axis]
    pairs = [(d, d ^ (bits << shift)) for d in range(lax.axis_size("dom"))]
    return lax.ppermute(block, "dom", pairs)


def moved_three(blocks, axis):
    return [move(blocks[i], axis, i) for i in (1, 2, 3)]


def total(own, near):
    return (own + near[0]) + (near[1] + near[2])


def shards(
    features,
    self_weight,
    neighbor_weight,
    tile_values,
    tile_row,
    tile_owner,
    send_tile,
    tile_count,
    hub_panel,
    hub_rows,
    cotangent,
):
    rows_dev, half = features.shape
    tile_edge = tile_values.shape[1]
    tiles_dev = rows_dev // tile_edge
    dom_size = lax.axis_size("dom")
    core = lax.axis_index("feat")

    outgoing = pack(features, send_tile, hub_rows, tile_edge)
    incoming = exchange(outgoing)

    def own_first(w):
        return jnp.where(core == 0, w, jnp.concatenate([w[:, half:], w[:, :half]], axis=1))

    weights = own_first(jnp.concatenate([self_weight, neighbor_weight], axis=0))
    peer_weights = swap(weights)
    peer_weights = jnp.concatenate([peer_weights[:, half:], peer_weights[:, :half]], axis=1)
    own_w = jnp.concatenate([weights[:half], peer_weights[:half]], axis=0)
    nbr_w = jnp.concatenate([weights[half:], peer_weights[half:]], axis=0)
    feat_peer = swap(features)
    cot_peer = swap(cotangent)

    by_owner, by_row, duos = plan(tile_row, tile_owner, tile_count, tiles_dev, dom_size)
    order, order_row, order_owner = by_owner
    first, second, kinds, pair_row, owner_a, owner_b, n_duos = by_row
    inv, flipped, pairs, panel_t = prepare(
        tile_row, tile_count, order, first, second, kinds, tile_values, hub_panel, duos,
        (own_w, nbr_w, feat_peer, cot_peer),
    )

    aggregate = gather(pair_row, owner_a, owner_b, n_duos, pairs, incoming, hub_panel, inv)
    agg_peer = swap(aggregate)
    terms = middle(
        order_row, order_owner, tile_count,
        features, feat_peer, aggregate, agg_peer, cotangent, cot_peer, inv, panel_t, flipped,
        own_w, nbr_w, dom_size,
    )
    returned = exchange(terms)

    where = jnp.stack([lax.axis_index("dom").astype(jnp.int32), core.astype(jnp.int32)])
    layer_out, slopes, grads = side(
        where, features, feat_peer, aggregate, agg_peer, cotangent, cot_peer, own_w, nbr_w, terms
    )
    grads = total(grads[0], moved_three(grads, "y"))
    direct, grads = direct_part(slopes, own_w[:half], grads)
    grads = total(grads, [move(grads, "x", i) for i in (1, 2, 3)])
    grads = total(grads, [move(grads, "z", i) for i in (1, 2, 3)])
    grads = grads + move(grads, "z", 4)
    near = [move(grads, "y", i) for i in (1, 2, 3)]
    input_grad, grads = finish(
        send_tile, hub_rows, returned, direct.reshape(tiles_dev, tile_edge, half), grads
    )
    input_grad = input_grad.reshape(rows_dev, half)
    self_grad, neighbor_grad = put_in_place(
        where, [grads] + near, 1.0 / math.sqrt(rows_dev * dom_size)
    )
    return (layer_out, self_grad, neighbor_grad, input_grad)


def solution(mesh):
    placed = (
        P("dom", "feat"),
        P("feat", None),
        P("feat", None),
        P("dom", None, None),
        P("dom"),
        P("dom"),
        P("dom"),
        P("dom"),
        P("dom", None),
        P("dom"),
        P("dom", "feat"),
    )
    return jax.shard_map(
        shards,
        mesh=mesh,
        in_specs=placed,
        out_specs=(P("dom", "feat"), P("feat", None), P("feat", None), P("dom", "feat")),
        check_vma=False,
    )
```

```python
import math

import jax
import jax.numpy as jnp
from jax import lax
from jax.experimental import pallas as pl
from jax.experimental.pallas import tpu as pltpu
from jax.sharding import PartitionSpec as P

F32 = jnp.float32
BF16 = jnp.bfloat16
MIB = 1 << 20


def dot(a, b, dims):
    return lax.dot_general(a, b, (dims, ((), ())), preferred_element_type=F32)


NN = ((1,), (0,))
NT = ((1,), (1,))
TN = ((0,), (0,))


def params(mib, steps):
    return pltpu.CompilerParams(
        dimension_semantics=("arbitrary",) * steps, vmem_limit_bytes=mib * MIB
    )


ANY = pl.BlockSpec(memory_space=pl.ANY)
HBM = pl.BlockSpec(memory_space=pltpu.HBM)
VMEM = pl.BlockSpec(memory_space=pltpu.VMEM)
SMEM = pl.BlockSpec(memory_space=pltpu.SMEM)


def own_copies(mib):
    return pltpu.CompilerParams(vmem_limit_bytes=mib * MIB)


def pack_kernel(send, hubs, feat, out, hub_rows, tails, sems):
    parts, height, width = out.shape
    edge = height - 8

    @pl.loop(0, parts // 8)
    def _(g):
        for i in range(8):
            q = g * 8 + i
            start = pl.multiple_of(send[q] * edge, edge)
            pltpu.make_async_copy(
                feat.at[pl.ds(start, edge), :], out.at[q, pl.ds(0, edge), :], sems.at[0]
            ).start()

    hub_rows[...] = jnp.zeros_like(hub_rows)
    for j in range(2):
        row = hubs[j]
        base = pl.multiple_of((row // 16) * 16, 16)
        block = feat[pl.ds(base, 16), :].astype(F32)
        here = lax.broadcasted_iota(jnp.int32, block.shape, 0) == row - base
        hub_rows[j : j + 1, :] = jnp.sum(jnp.where(here, block, 0.0), axis=0, keepdims=True)
    tails[...] = jnp.broadcast_to(hub_rows[...].astype(BF16)[None], tails.shape)
    tail = out.at[:, pl.ds(edge, 8), :]
    pltpu.make_async_copy(tails, tail, sems.at[1]).start()
    pltpu.make_async_copy(tails, tail, sems.at[1]).wait()
    body = out.at[:, pl.ds(0, edge), :]
    pltpu.make_async_copy(body, body, sems.at[0]).wait()


def pack(features, send_tile, hub_rows, edge):
    rows, width = features.shape
    parts = send_tile.shape[0]
    return pl.pallas_call(
        pack_kernel,
        name="pack",
        out_shape=jax.ShapeDtypeStruct((parts, edge + 8, width), BF16),
        grid_spec=pltpu.PrefetchScalarGridSpec(
            num_scalar_prefetch=2,
            grid=(1,),
            in_specs=[pl.BlockSpec((rows, width), lambda g, *_: (0, 0))],
            out_specs=HBM,
            scratch_shapes=[
                pltpu.VMEM((8, width), F32),
                pltpu.VMEM((parts, 8, width), BF16),
                pltpu.SemaphoreType.DMA((2,)),
            ],
        ),
        compiler_params=own_copies(58),
    )(send_tile, hub_rows, features)


def prepare_kernel(
    row, count, order, first, second, kinds, values, panel, *rest
):
    inv, flipped, pairs, panel_t, squares = rest[-5:]
    step, steps = pl.program_id(0), pl.num_programs(0)
    edge = values.shape[1]
    slots, duos = flipped.shape[0], pairs.shape[0]

    @pl.when(step == 0)
    def _():
        squares[...] = jnp.zeros_like(squares)

    @pl.loop(0, slots)
    def _(i):
        k = step * slots + i
        flipped[i] = values[order[k]].T
        tile = values[k].astype(F32)
        live = (k < count[0]).astype(F32)
        start = pl.multiple_of(row[k] * edge, edge)
        squares[pl.ds(start, edge), :] += tile * tile * live

    @pl.loop(0, duos)
    def _(i):
        p = step * duos + i
        has_first = (kinds[p] > 0).astype(BF16)
        has_second = (kinds[p] > 1).astype(BF16)
        pairs[i, :, :edge] = values[first[p]] * has_first
        pairs[i, :, edge:] = values[second[p]] * has_second

    @pl.when(step == steps - 1)
    def _():
        @pl.loop(0, squares.shape[0] // edge)
        def _(t):
            at = pl.ds(pl.multiple_of(t * edge, edge), edge)
            panel_t[:, at] = panel[at, :].T
            wide = panel[at, :].astype(F32)
            wide = wide * wide
            half = wide.shape[1] // 2
            total = jnp.sum(
                squares[at, :] + wide[:, :half] + wide[:, half:], axis=1, keepdims=True
            )
            inv[at, :] = jnp.broadcast_to(lax.rsqrt(1.0 + total), (edge, inv.shape[1]))


def prepare(row, count, order, first, second, kinds, values, panel, duos, ready):
    slots, edge, _ = values.shape
    rows, hubs = panel.shape
    steps = 4
    whole = lambda g, *_: (0, 0)
    return pl.pallas_call(
        prepare_kernel,
        name="prepare",
        out_shape=(
            jax.ShapeDtypeStruct((rows, edge), F32),
            jax.ShapeDtypeStruct((slots, edge, edge), BF16),
            jax.ShapeDtypeStruct((duos, edge, 2 * edge), BF16),
            jax.ShapeDtypeStruct((hubs, rows), BF16),
        ),
        grid_spec=pltpu.PrefetchScalarGridSpec(
            num_scalar_prefetch=6,
            grid=(steps,),
            in_specs=[
                pl.BlockSpec((slots, edge, edge), lambda g, *_: (0, 0, 0)),
                pl.BlockSpec((rows, hubs), whole),
            ]
            + [ANY] * len(ready),
            out_specs=(
                pl.BlockSpec((rows, edge), whole),
                pl.BlockSpec((slots // steps, edge, edge), lambda g, *_: (g, 0, 0)),
                pl.BlockSpec((duos // steps, edge, 2 * edge), lambda g, *_: (g, 0, 0)),
                pl.BlockSpec((hubs, rows), whole),
            ),
            scratch_shapes=[pltpu.VMEM((rows, edge), F32)],
        ),
        compiler_params=params(40, 1),
        cost_estimate=pl.CostEstimate(
            flops=60_000_000_000, bytes_accessed=40_000_000, transcendentals=0
        ),
    )(row, count, order, first, second, kinds, values, panel, *ready)


DUO_STEP = 16


def gather_kernel(
    row, owner_a, owner_b, n_duos, pairs, incoming, panel, inv, out,
    tail, pan, tiles, norm, duos, tail_wide, hub_wide, sums, result, sems, duo_sems, out_sems,
):
    parts, edge, _ = tiles.shape
    rows = sums.shape[0]
    copy = pltpu.make_async_copy
    tail_in = copy(incoming.at[:, pl.ds(edge, 8), :], tail, sems.at[0])
    panel_in = copy(panel, pan, sems.at[1])
    tiles_in = copy(incoming.at[:, pl.ds(0, edge), :], tiles, sems.at[2])
    norm_in = copy(inv, norm, sems.at[3])
    steps = duos.shape[0] // DUO_STEP
    duo_in = [
        copy(pairs.at[pl.ds(c * DUO_STEP, DUO_STEP)], duos.at[pl.ds(c * DUO_STEP, DUO_STEP)], duo_sems.at[c])
        for c in range(steps)
    ]
    tail_in.start()
    panel_in.start()
    tiles_in.start()
    for c in range(steps):

        @pl.when(c * DUO_STEP < n_duos[0])
        def _():
            duo_in[c].start()

    norm_in.start()

    tail_in.wait()
    tail_wide[...] = tail[...].reshape(tail_wide.shape).astype(F32)
    for j in range(2):
        hub_wide[pl.ds(j, parts, stride=2), :] = tail_wide[pl.ds(j, parts, stride=8), :]
    hub_feats = hub_wide[...].astype(BF16)
    panel_in.wait()
    block = 512
    for t in range(rows // block):
        at = pl.ds(t * block, block)
        sums[at, :] = dot(pan[at, :], hub_feats, NN)
    tiles_in.wait()
    for c in range(steps):

        @pl.when(c * DUO_STEP < n_duos[0])
        def _():
            duo_in[c].wait()
            products = []
            for i in range(DUO_STEP):
                p = c * DUO_STEP + i
                columns = jnp.concatenate([tiles[owner_a[p]], tiles[owner_b[p]]], axis=0)
                products.append(dot(duos[p], columns, NN))
            for i in range(DUO_STEP):
                start = pl.multiple_of(row[c * DUO_STEP + i] * edge, edge)
                sums[pl.ds(start, edge), :] += products[i]

    norm_in.wait()
    block = rows // 4
    sent = []
    for t in range(4):
        at = pl.ds(t * block, block)
        result[at, :] = (sums[at, :] * norm[at, :]).astype(BF16)
        sent.append(copy(result.at[at, :], out.at[at, :], out_sems.at[t]))
        sent[-1].start()
    for s in sent:
        s.wait()


def gather(row, owner_a, owner_b, n_duos, pairs, incoming, panel, inv):
    duos, edge, _ = pairs.shape
    rows, hubs = panel.shape
    parts = incoming.shape[0]
    return pl.pallas_call(
        gather_kernel,
        name="gather",
        out_shape=jax.ShapeDtypeStruct((rows, edge), BF16),
        grid_spec=pltpu.PrefetchScalarGridSpec(
            num_scalar_prefetch=4,
            grid=(1,),
            in_specs=[ANY] * 4,
            out_specs=HBM,
            scratch_shapes=[
                pltpu.VMEM((parts, 8, edge), BF16),
                pltpu.VMEM((rows, hubs), BF16),
                pltpu.VMEM((parts, edge, edge), BF16),
                pltpu.VMEM((rows, edge), F32),
                pltpu.VMEM(pairs.shape, BF16),
                pltpu.VMEM((parts * 8, edge), F32),
                pltpu.VMEM((hubs, edge), F32),
                pltpu.VMEM((rows, edge), F32),
                pltpu.VMEM((rows, edge), BF16),
                pltpu.SemaphoreType.DMA((4,)),
                pltpu.SemaphoreType.DMA((duos // DUO_STEP,)),
                pltpu.SemaphoreType.DMA((4,)),
            ],
        ),
        compiler_params=own_copies(58),
    )(row, owner_a, owner_b, n_duos, pairs, incoming, panel, inv)


ROW_STEPS = 4
MID_MIB = 56
SLOT_STEP = 16


def middle_kernel(
    order_row, order_owner, count,
    feat, feat_peer, agg, agg_peer, cot, cot_peer, inv, panel_t, flipped, own_w, nbr_w,
    terms,
    feat_v, feat_peer_v, agg_v, agg_peer_v, cot_v, cot_peer_v, inv_v, panel_v, flipped_v,
    agg_slopes, terms_v, hub_acc, hub_wide, carry, in_sems, flip_sems, term_sems,
):
    rows, half = feat_v.shape
    slots, edge, _ = flipped_v.shape
    parts = terms_v.shape[0]
    copy = pltpu.make_async_copy
    block = rows // ROW_STEPS
    sources = (feat, feat_peer, agg, agg_peer, cot, cot_peer, inv)
    places = (feat_v, feat_peer_v, agg_v, agg_peer_v, cot_v, cot_peer_v, inv_v)
    at = [pl.ds(t * block, block) for t in range(ROW_STEPS)]
    inputs = [
        [copy(s.at[at[t], :], d.at[at[t], :], in_sems.at[t, i]) for i, (s, d) in enumerate(zip(sources, places))]
        + [copy(panel_t.at[:, at[t]], panel_v.at[:, at[t]], in_sems.at[t, 7])]
        for t in range(ROW_STEPS)
    ]
    steps = slots // SLOT_STEP
    flips = [
        copy(flipped.at[pl.ds(b * SLOT_STEP, SLOT_STEP)], flipped_v.at[pl.ds(b * SLOT_STEP, SLOT_STEP)], flip_sems.at[b])
        for b in range(steps)
    ]
    for t in range(ROW_STEPS):
        for c in inputs[t]:
            c.start()
    for b in range(steps):

        @pl.when(b * SLOT_STEP < count[0])
        def _():
            flips[b].start()

    terms_v[:, :edge, :] = jnp.zeros((parts, edge, half), BF16)
    hub_wide[...] = jnp.zeros_like(hub_wide)
    carry[...] = jnp.zeros_like(carry)

    for t in range(ROW_STEPS):
        for c in inputs[t]:
            c.wait()
        here = at[t]
        preact = dot(
            jnp.concatenate([feat_v[here, :], feat_peer_v[here, :]], axis=1), own_w[...], NN
        ) + dot(jnp.concatenate([agg_v[here, :], agg_peer_v[here, :]], axis=1), nbr_w[...], NN)
        cotangent = jnp.concatenate([cot_v[here, :], cot_peer_v[here, :]], axis=1).astype(F32)
        slope = jnp.where(preact > 0, cotangent, 0.0).astype(BF16)
        back = (dot(slope, nbr_w[:half, :], NT) * inv_v[here, :]).astype(BF16)
        agg_slopes[here, :] = back
        hub = dot(panel_v[:, here], back, NN)
        if t == 0:
            hub_acc[...] = hub
        else:
            hub_acc[...] += hub

    for j in range(2):
        hub_wide[pl.ds(j, parts, stride=8), :] = hub_acc[pl.ds(j, parts, stride=2), :]
    terms_v[:, edge:, :] = hub_wide[...].reshape(parts, 8, half).astype(BF16)

    group = parts // 8
    for b in range(steps):

        @pl.when(b * SLOT_STEP < count[0])
        def _():
            flips[b].wait()
            products = []
            for i in range(SLOT_STEP):
                k = b * SLOT_STEP + i
                start = pl.multiple_of(order_row[k] * edge, edge)
                products.append(dot(flipped_v[k], agg_slopes[pl.ds(start, edge), :], NN))
            total = carry[...]
            for i in range(SLOT_STEP):
                k = b * SLOT_STEP + i
                live = (k < count[0]).astype(F32)
                fresh = products[i] * live
                if k:
                    same = (order_owner[k] == order_owner[k - 1]).astype(F32)
                    total = fresh + total * same
                else:
                    total = fresh
                terms_v[order_owner[k], :edge, :] = total.astype(BF16)
            carry[...] = total
            first = order_owner[b * SLOT_STEP] // group if b else 0
            after = (b + 1) * SLOT_STEP
            last = jnp.where(
                after >= count[0], parts // group, order_owner[min(after, slots - 1)] // group
            )

            @pl.loop(first, last)
            def _(g):
                owners = pl.ds(g * group, group)
                copy(terms_v.at[owners], terms.at[owners], term_sems.at[0]).start()

    copy(terms_v, terms, term_sems.at[0]).wait()


def middle(
    order_row, order_owner, count,
    feat, feat_peer, agg, agg_peer, cot, cot_peer, inv, panel_t, flipped, own_w, nbr_w, parts,
):
    rows, half = feat.shape
    hubs = panel_t.shape[0]
    edge = flipped.shape[1]
    narrow = pltpu.VMEM((rows, half), BF16)
    whole = lambda g, *_: (0, 0)
    height = edge + 8
    return pl.pallas_call(
        middle_kernel,
        name="middle",
        out_shape=jax.ShapeDtypeStruct((parts, height, half), BF16),
        grid_spec=pltpu.PrefetchScalarGridSpec(
            num_scalar_prefetch=3,
            grid=(1,),
            in_specs=[ANY] * 9
            + [pl.BlockSpec(own_w.shape, whole), pl.BlockSpec(nbr_w.shape, whole)],
            out_specs=HBM,
            scratch_shapes=[narrow] * 6
            + [
                pltpu.VMEM((rows, half), F32),
                pltpu.VMEM((hubs, rows), BF16),
                pltpu.VMEM(flipped.shape, BF16),
                narrow,
                pltpu.VMEM((parts, height, half), BF16),
                pltpu.VMEM((hubs, half), F32),
                pltpu.VMEM((4 * hubs, half), F32),
                pltpu.VMEM((edge, half), F32),
                pltpu.SemaphoreType.DMA((ROW_STEPS, 8)),
                pltpu.SemaphoreType.DMA((flipped.shape[0] // SLOT_STEP,)),
                pltpu.SemaphoreType.DMA((1,)),
            ],
        ),
        compiler_params=own_copies(MID_MIB),
    )(
        order_row, order_owner, count,
        feat, feat_peer, agg, agg_peer, cot, cot_peer, inv, panel_t, flipped, own_w, nbr_w,
    )


def side_kernel(
    where, feat, feat_peer, agg, agg_peer, cot, cot_peer, own_w, nbr_w, layer, slopes, grads, acc
):
    step, steps = pl.program_id(0), pl.num_programs(0)
    half = feat.shape[1]
    x, a = feat[...], agg[...]
    preact = dot(jnp.concatenate([x, feat_peer[...]], axis=1), own_w[...], NN) + dot(
        jnp.concatenate([a, agg_peer[...]], axis=1), nbr_w[...], NN
    )
    layer[...] = jnp.maximum(preact[:, :half], 0.0).astype(BF16)
    cotangent = jnp.concatenate([cot[...], cot_peer[...]], axis=1).astype(F32)
    slope = jnp.where(preact > 0, cotangent, 0.0).astype(BF16)
    slopes[...] = slope
    part = dot(jnp.concatenate([x, a], axis=1), slope, TN)

    @pl.when(step == 0)
    def _():
        acc[...] = part

    @pl.when(step > 0)
    def _():
        acc[...] += part

    @pl.when(step == steps - 1)
    def _():
        y = where[0] % 4
        for c in range(4):
            grads[jnp.bitwise_xor(c, y)] = acc[
                (c // 2) * half : (c // 2 + 1) * half, (c % 2) * half : (c % 2 + 1) * half
            ]


def side(where, feat, feat_peer, agg, agg_peer, cot, cot_peer, own_w, nbr_w, after):
    rows, half = feat.shape
    block = rows // ROW_STEPS
    by_row = lambda width: pl.BlockSpec((block, width), lambda g, *_: (g, 0))
    whole = lambda g, *_: (0, 0)
    return pl.pallas_call(
        lambda *refs: side_kernel(*refs[:9], *refs[10:]),
        name="side",
        out_shape=(
            jax.ShapeDtypeStruct((rows, half), BF16),
            jax.ShapeDtypeStruct((rows, 2 * half), BF16),
            jax.ShapeDtypeStruct((4, half, half), F32),
        ),
        grid_spec=pltpu.PrefetchScalarGridSpec(
            num_scalar_prefetch=1,
            grid=(rows // block,),
            in_specs=[by_row(half)] * 6
            + [pl.BlockSpec(own_w.shape, whole), pl.BlockSpec(nbr_w.shape, whole), ANY],
            out_specs=(
                by_row(half),
                by_row(2 * half),
                pl.BlockSpec((4, half, half), lambda g, *_: (0, 0, 0)),
            ),
            scratch_shapes=[pltpu.VMEM((2 * half, 2 * half), F32)],
        ),
        compiler_params=params(32, 1),
    )(where, feat, feat_peer, agg, agg_peer, cot, cot_peer, own_w, nbr_w, after)


def direct_kernel(slopes, own_w, passed, direct, passed_out):
    passed_out[...] = passed[...]
    block = 512
    for t in range(slopes.shape[0] // block):
        at = pl.ds(t * block, block)
        direct[at, :] = dot(slopes[at, :], own_w[...], NT)


def direct_part(slopes, own_w, passed):
    return pl.pallas_call(
        direct_kernel,
        name="direct",
        out_shape=(
            jax.ShapeDtypeStruct((slopes.shape[0], own_w.shape[0]), F32),
            jax.ShapeDtypeStruct(passed.shape, passed.dtype),
        ),
        in_specs=[VMEM] * 3,
        out_specs=(VMEM, VMEM),
        compiler_params=own_copies(8),
    )(slopes, own_w, passed)


def finish_kernel(
    send, hubs, returned, direct, grads, out, grads_out, acc, landed, sems, part_sems
):
    parts, height, half = landed.shape
    edge = acc.shape[1]
    copy = pltpu.make_async_copy
    steps = 4
    group = parts // steps
    arrivals = [
        copy(returned.at[pl.ds(g * group, group)], landed.at[pl.ds(g * group, group)], part_sems.at[g])
        for g in range(steps)
    ]
    for c in arrivals:
        c.start()
    grads_out[...] = grads[...]
    acc[...] = direct[...]
    share = jnp.zeros((8, half), F32)
    for g in range(steps):
        arrivals[g].wait()
        for i in range(group):
            p = g * group + i
            acc[send[p]] += landed[p, :edge, :].astype(F32)
            share = share + landed[p, edge:, :].astype(F32)
    for j in range(2):
        row = hubs[j]
        tile, inside = row // edge, row % edge
        base = pl.multiple_of((inside // 8) * 8, 8)
        here = lax.broadcasted_iota(jnp.int32, (8, half), 0) == inside - base
        acc[tile, pl.ds(base, 8), :] += jnp.where(here, share[j : j + 1, :], 0.0)
    end = copy(acc, out, sems.at[0])
    end.start()
    end.wait()


def finish(send_tile, hub_rows, returned, direct, grads):
    return pl.pallas_call(
        finish_kernel,
        name="finish",
        out_shape=(
            jax.ShapeDtypeStruct(direct.shape, F32),
            jax.ShapeDtypeStruct(grads.shape, F32),
        ),
        in_specs=[SMEM, SMEM, ANY, VMEM, VMEM],
        out_specs=(HBM, VMEM),
        scratch_shapes=[
            pltpu.VMEM(direct.shape, F32),
            pltpu.VMEM(returned.shape, BF16),
            pltpu.SemaphoreType.DMA((1,)),
            pltpu.SemaphoreType.DMA((4,)),
        ],
        compiler_params=own_copies(16),
    )(send_tile, hub_rows, returned, direct, grads)


def place_kernel(factor, where, own, one, two, three, self_grad, neighbor_grad, blocks):
    for m, group in enumerate((own, one, two, three)):
        blocks[m] = group[...]
    y, core = where[0] % 4, where[1]
    half = blocks.shape[2]
    for j, out in enumerate((self_grad, neighbor_grad)):
        for c in range(2):
            column = 2 * j + jnp.bitwise_xor(c, core)
            out[:, c * half : (c + 1) * half] = blocks[jnp.bitwise_xor(column, y)] * factor


def put_in_place(where, groups, factor):
    rows, half = groups[0].shape
    out = jax.ShapeDtypeStruct((rows, 2 * half), F32)
    return pl.pallas_call(
        lambda *refs: place_kernel(factor, *refs),
        name="place",
        out_shape=(out, out),
        in_specs=[SMEM] + [VMEM] * 4,
        out_specs=(VMEM, VMEM),
        scratch_shapes=[pltpu.VMEM((4, rows, half), F32)],
        compiler_params=own_copies(8),
    )(where, *groups)


def plan(tile_row, tile_owner, tile_count, tiles, parts):
    slots = tile_row.shape[0]
    index = jnp.arange(slots, dtype=jnp.int32)
    live = index < tile_count[0]
    earlier = index[None, :] < index[:, None]
    pick = lambda where, what: jnp.sum(jnp.where(where, what, 0), axis=1, dtype=jnp.int32)

    key = jnp.where(live, tile_owner, parts)
    before = (key[None, :] < key[:, None]) | ((key[None, :] == key[:, None]) & earlier)
    rank = jnp.sum(before, axis=1, dtype=jnp.int32)
    last = jnp.minimum(index, tile_count[0] - 1)
    at = rank[None, :] == last[:, None]
    order = pick(at, index[None, :])
    order_row = pick(at, tile_row[None, :])
    order_owner = pick(at, tile_owner[None, :])

    mates = live[None, :] & (tile_row[None, :] == tile_row[:, None])
    inside = jnp.sum(mates & earlier, axis=1, dtype=jnp.int32)
    rows = jnp.arange(tiles, dtype=jnp.int32)
    per_row = jnp.sum(live[None, :] & (tile_row[None, :] == rows[:, None]), axis=1, dtype=jnp.int32)
    row_pairs = (per_row + 1) // 2
    lower = jnp.sum(
        jnp.where(rows[None, :] < tile_row[:, None], row_pairs[None, :], 0), axis=1, dtype=jnp.int32
    )
    pair = jnp.where(live, lower + inside // 2, -1)
    duos = (slots + tiles) // 2
    p = jnp.arange(duos, dtype=jnp.int32)
    is_first = (pair[None, :] == p[:, None]) & (inside[None, :] % 2 == 0)
    is_second = (pair[None, :] == p[:, None]) & (inside[None, :] % 2 == 1)
    first = pick(is_first, index[None, :])
    second = pick(is_second, index[None, :])
    owner_a = pick(is_first, tile_owner[None, :])
    owner_b = pick(is_second, tile_owner[None, :])
    pair_row = pick(is_first, tile_row[None, :])
    kinds = pick(is_first, 1) + pick(is_second, 1)
    n_duos = jnp.sum(row_pairs, dtype=jnp.int32).reshape(1)
    return (
        (order, order_row, order_owner),
        (first, second, kinds, pair_row, owner_a, owner_b, n_duos),
        duos,
    )


def exchange(block):
    return lax.all_to_all(block, "dom", split_axis=0, concat_axis=0, tiled=True)


def swap(block):
    return lax.ppermute(block, "feat", [(0, 1), (1, 0)])


def move(block, axis, bits):
    shift = {"z": 4, "x": 2, "y": 0}[axis]
    pairs = [(d, d ^ (bits << shift)) for d in range(lax.axis_size("dom"))]
    return lax.ppermute(block, "dom", pairs)


def moved_three(blocks, axis):
    return [move(blocks[i], axis, i) for i in (1, 2, 3)]


def total(own, near):
    return (own + near[0]) + (near[1] + near[2])


def shards(
    features,
    self_weight,
    neighbor_weight,
    tile_values,
    tile_row,
    tile_owner,
    send_tile,
    tile_count,
    hub_panel,
    hub_rows,
    cotangent,
):
    rows_dev, half = features.shape
    tile_edge = tile_values.shape[1]
    tiles_dev = rows_dev // tile_edge
    dom_size = lax.axis_size("dom")
    core = lax.axis_index("feat")

    outgoing = pack(features, send_tile, hub_rows, tile_edge)
    incoming = exchange(outgoing)

    def own_first(w):
        return jnp.where(core == 0, w, jnp.concatenate([w[:, half:], w[:, :half]], axis=1))

    weights = own_first(jnp.concatenate([self_weight, neighbor_weight], axis=0))
    peer_weights = swap(weights)
    peer_weights = jnp.concatenate([peer_weights[:, half:], peer_weights[:, :half]], axis=1)
    own_w = jnp.concatenate([weights[:half], peer_weights[:half]], axis=0)
    nbr_w = jnp.concatenate([weights[half:], peer_weights[half:]], axis=0)
    feat_peer = swap(features)
    cot_peer = swap(cotangent)

    by_owner, by_row, duos = plan(tile_row, tile_owner, tile_count, tiles_dev, dom_size)
    order, order_row, order_owner = by_owner
    first, second, kinds, pair_row, owner_a, owner_b, n_duos = by_row
    inv, flipped, pairs, panel_t = prepare(
        tile_row, tile_count, order, first, second, kinds, tile_values, hub_panel, duos,
        (own_w, nbr_w, feat_peer, cot_peer),
    )

    aggregate = gather(pair_row, owner_a, owner_b, n_duos, pairs, incoming, hub_panel, inv)
    agg_peer = swap(aggregate)
    terms = middle(
        order_row, order_owner, tile_count,
        features, feat_peer, aggregate, agg_peer, cotangent, cot_peer, inv, panel_t, flipped,
        own_w, nbr_w, dom_size,
    )
    returned = exchange(terms)

    where = jnp.stack([lax.axis_index("dom").astype(jnp.int32), core.astype(jnp.int32)])
    layer_out, slopes, grads = side(
        where, features, feat_peer, aggregate, agg_peer, cotangent, cot_peer, own_w, nbr_w, terms
    )
    grads = total(grads[0], moved_three(grads, "y"))
    direct, grads = direct_part(slopes, own_w[:half], grads)
    grads = total(grads, [move(grads, "x", i) for i in (1, 2, 3)])
    grads = total(grads, [move(grads, "z", i) for i in (1, 2, 3)])
    far = move(grads, "z", 4)
    input_grad, grads = finish(
        send_tile, hub_rows, returned, direct.reshape(tiles_dev, tile_edge, half), grads
    )
    input_grad = input_grad.reshape(rows_dev, half)
    grads = grads + far
    near = [move(grads, "y", i) for i in (1, 2, 3)]
    self_grad, neighbor_grad = put_in_place(
        where, [grads] + near, 1.0 / math.sqrt(rows_dev * dom_size)
    )
    return (layer_out, self_grad, neighbor_grad, input_grad)


def solution(mesh):
    placed = (
        P("dom", "feat"),
        P("feat", None),
        P("feat", None),
        P("dom", None, None),
        P("dom"),
        P("dom"),
        P("dom"),
        P("dom"),
        P("dom", None),
        P("dom"),
        P("dom", "feat"),
    )
    return jax.shard_map(
        shards,
        mesh=mesh,
        in_specs=placed,
        out_specs=(P("dom", "feat"), P("feat", None), P("feat", None), P("dom", "feat")),
        check_vma=False,
    )
```
